32 devices in a mesh: section: 4 (over y, x), student: 2 (over core), dp: 4 (over z).
Axes of the slice: x: 2, y: 2, z: 4, core: 2. Of those that a mesh axis runs over, the one named last changes fastest.
Arguments:
- in_flight: bfloat16 [4, 2, 128, 4096], P('section', 'student'), may hold values from -6 to 6
- segments: int32 [4, 2, 128], P(None, 'student'), may hold values from 0 to 3, never falling along the last dimension, each value on 1 to 64 neighbouring positions
- norm_gain: float32 [4, 4096], P('section'), may hold values from 0.5 to 1.5
- w_qkv: bfloat16 [4, 4096, 3, 1024], P('section', None, None, 'dp')
- w_out: bfloat16 [4, 1024, 4096], P('section', 'dp'), may hold values from -0.1875 to 0.1875
- final_gain: float32 [4096], replicated, may hold values from 0.25 to 1.75
- student_rows: bfloat16 [2, 3, 2, 128, 1024], P('student', None, None, 'dp'), may hold values from -6 to 6
- student_gain: float32 [2, 1024], P('student'), may hold values from 0.5 to 1.5
- w_head: bfloat16 [2, 1024, 4096], P('student', None, 'section'), may hold values from -0.1875 to 0.1875
Outputs:
- advanced: bfloat16 [4, 2, 128, 4096], P('section', 'student', 'dp')
- grad_head: float32 [2, 1024, 4096], P('student', 'dp', 'section')
The draws below stay inside these ranges and needn't reach their ends.
Inputs may be any that keep to these rules, and one draw needn't show every extreme that they name: `segments`: along a micro-batch's tokens the crop numbers never fall; each of the 4 crops holds 1 to 64 tokens and one holds exactly 64.
All inputs are finite; a program needn't handle non-finite values.
Results may differ from the reference program's by a relative error of at most 0.025.
Values may be sent and summed in bfloat16 or wider, within the bound.
A program may use at most 64 MiB of HBM per device.

```python
import math
import jax
import jax.numpy as jnp
import numpy as np
from jax import lax

D = 4096
HEAD_SIZE = 128
SW = 1024
TOK = 128
TICKS = 3
CROPS = 4
CROP_MOST = 64
HEADS = 8
SECTIONS = 4
COLS = 2
GROUPS = 2
N_DP = 4


def draw_w_qkv(key, part):
    first = jax.random.fold_in(key, 11)
    width = HEADS * HEAD_SIZE
    base = jax.random.truncated_normal(first, -6.0, 6.0, (SECTIONS, D, 3, width), jnp.float32) * D ** (-0.5)
    return base.astype(jnp.bfloat16)


def raised(result, stream_key, source, target, blocks, factor):
    owner, partner = [(jnp.arange(result.shape[axis_at]) // (result.shape[axis_at] // blocks)).reshape([-1 if axis == axis_at else 1 for axis in range(result.ndim)]) for axis_at in (source, target)]
    chosen = jax.random.permutation(stream_key, blocks)[partner]
    strong = (owner == chosen) | (owner == (partner + blocks // 2) % blocks)
    return jnp.where(strong, factor * result, result)


def block_levels(own_key, extent, pieces, smallest, high):
    loudness, own = 1.0, jax.random.fold_in(own_key, 6)
    for axis_at, parts in pieces:
        heights = jnp.exp(jax.random.uniform(jax.random.fold_in(own, axis_at), (parts,), jnp.float32, smallest / len(pieces), high / len(pieces)))
        loudness = loudness * jnp.repeat(heights, extent[axis_at] // parts).reshape([-1 if axis == axis_at else 1 for axis in range(len(extent))])
    return loudness


def length_profile(amount, total, bound, lean):
    portions = [(1 << 20) // math.isqrt(standing ** lean) + 1 for standing in range(2, amount + 1)]
    spare, given = total - bound - (amount - 1), [1] * (amount - 1)
    while spare > 0:
        free = [i for i in range(amount - 1) if given[i] < bound]
        mass, budget = sum([portions[i] for i in free]), spare
        for i in free:
            extra = min(bound - given[i], max(1, budget * portions[i] // mass), spare)
            given[i] = given[i] + extra
            spare = spare - extra
    return np.array([bound] + given)


def ragged_sizes(stream_key, number_of, total, bound, skew):
    if number_of == 2:
        one = jax.random.randint(stream_key, (), max(1, total - bound), min(bound, total - 1) + 1)
        return jnp.stack([one, total - one])
    sizes = jnp.asarray(length_profile(number_of, total, bound, skew), jnp.int32)
    couples = (number_of - 1) // 2
    giver, receiver = sizes[1:1 + 2 * couples:2], sizes[2:2 + 2 * couples:2]
    margin = jnp.minimum(giver - 1, bound - receiver)
    moved = jax.random.randint(jax.random.fold_in(stream_key, 1), (couples,), 0, 1 << 20) % (margin + 1)
    sizes = sizes.at[1:1 + 2 * couples:2].set(giver - moved).at[2:2 + 2 * couples:2].set(receiver + moved)
    return sizes[jax.random.permutation(jax.random.fold_in(stream_key, 2), number_of)]


def normal_values(stream_key, dims, scale, most, shards=(), kind=jnp.bfloat16):
    entries = scale * jax.random.normal(stream_key, dims, jnp.float32)
    if shards:
        entries = entries * block_levels(stream_key, dims, shards, -0.22, 0.18)
    return jnp.clip(entries, -most, most).astype(kind)


def noise_with(rng, extent, scale, reach, shards, heavy, dtype=jnp.bfloat16):
    drawn = scale * jax.random.normal(rng, extent, jnp.float32)
    if shards:
        drawn = drawn * block_levels(rng, extent, shards, -0.22, 0.18)
    return jnp.clip(raised(drawn, jax.random.fold_in(rng, 3), *heavy), -reach, reach).astype(dtype)


def setup_inputs(seed: int = 0) -> dict:
    splits = jax.random.split(jax.random.key(seed), 10)
    return {
        "in_flight": normal_values(splits[0], (SECTIONS, COLS, TOK, D), 1.0, 6.0, ((0, 4), (1, 2))),
        "segments": jax.vmap(lambda own: jnp.searchsorted(jnp.cumsum(ragged_sizes(own, CROPS, TOK, CROP_MOST, 1)), jnp.arange(TOK), side="right"))(jax.random.split(splits[1], SECTIONS * COLS)).reshape((SECTIONS, COLS, TOK)).astype(jnp.int32),
        "norm_gain": jnp.clip(1.0 + 0.1 * jax.random.normal(splits[2], (SECTIONS, D), jnp.float32), 0.5, 1.5),
        "w_qkv": draw_w_qkv(jax.random.fold_in(splits[9], 71), 0),
        "w_out": normal_values(splits[4], (SECTIONS, HEADS * HEAD_SIZE, D), (HEADS * HEAD_SIZE) ** -0.5, 0.1875, ((0, 4), (1, 4))),
        "final_gain": jnp.clip(1.0 + 0.15 * jax.random.normal(splits[5], (D,), jnp.float32), 0.25, 1.75),
        "student_rows": noise_with(splits[6], (GROUPS, TICKS, COLS, TOK, SW), 1.0, 6.0, ((0, 2), (3, 4)), (3, 4, 4, 2.0)),
        "student_gain": jnp.clip(1.0 + 0.1 * jax.random.normal(splits[7], (GROUPS, SW), jnp.float32), 0.5, 1.5),
        "w_head": normal_values(splits[8], (GROUPS, SW, D), SW ** -0.5, 0.1875, ((0, 2), (2, 4))),
    }


def layer_norm(rows, gain):
    rows = rows.astype(jnp.float32)
    centred = rows - lax.optimization_barrier(jnp.mean(rows, axis=-1, keepdims=True))
    spread = lax.optimization_barrier(jnp.mean(centred * centred, axis=-1, keepdims=True))
    return centred * lax.rsqrt(spread + 1e-06) * gain.astype(jnp.float32)

def teacher_layer(state, crops, gain, weights_qkv, weights_out):
    tokens = state.shape[0]
    width = weights_out.shape[0]
    heads = width // HEAD_SIZE
    normed = layer_norm(state, gain).astype(jnp.bfloat16)
    qkv = jnp.dot(normed, weights_qkv.reshape(weights_qkv.shape[0], 3 * width), preferred_element_type=jnp.float32).astype(jnp.bfloat16)
    query = qkv[:, :width].reshape(tokens, heads, HEAD_SIZE).astype(jnp.float32)
    keys = qkv[:, width:2 * width].reshape(tokens, heads, HEAD_SIZE).astype(jnp.float32)
    values = qkv[:, 2 * width:].reshape(tokens, heads, HEAD_SIZE).astype(jnp.float32)
    scores = jnp.einsum('qhd,khd->hqk', query, keys) * HEAD_SIZE ** (-0.5)
    same = crops[:, None] == crops[None, :]
    scores = jnp.where(same[None], scores, -1e+30)
    top = lax.optimization_barrier(jnp.max(scores, axis=-1, keepdims=True))
    expo = jnp.exp(scores - top)
    probs = (expo / lax.optimization_barrier(jnp.sum(expo, axis=-1, keepdims=True))).astype(jnp.bfloat16)
    mixed = jnp.einsum('hqk,khd->qhd', probs.astype(jnp.float32), values).astype(jnp.bfloat16).reshape(tokens, width)
    part = width // N_DP
    partials = jnp.einsum('tjc,jcd->jtd', mixed.reshape(tokens, N_DP, part).astype(jnp.float32), weights_out.reshape(N_DP, part, -1).astype(jnp.float32))
    partials = lax.optimization_barrier(partials.astype(jnp.bfloat16)).astype(jnp.float32)
    return (state.astype(jnp.float32) + lax.optimization_barrier(jnp.sum(partials, axis=0))).astype(jnp.bfloat16)

def reference(in_flight, segments, norm_gain, w_qkv, w_out, final_gain, student_rows, student_gain, w_head):
    sections = in_flight.shape[0]
    layer = jax.vmap(teacher_layer, in_axes=(0, 0, None, None, None))
    advanced = jnp.zeros_like(in_flight)
    finished = [None] * TICKS
    for start in range(sections):
        state = in_flight[start]
        for tick in range(TICKS):
            where = start + tick
            if where < sections:
                state = layer(state, segments[start], norm_gain[where], w_qkv[where], w_out[where])
                if where == sections - 1:
                    finished[tick] = layer_norm(state, final_gain).astype(jnp.bfloat16)
        if start + TICKS < sections:
            advanced = advanced.at[start + TICKS].set(state)
    targets = jnp.stack(finished).astype(jnp.float32)
    share = TOK // N_DP
    grads = []
    for member in range(student_rows.shape[0]):
        feats = layer_norm(student_rows[member], student_gain[member]).astype(jnp.bfloat16)
        pred = jnp.einsum('tcns,sd->tcnd', feats.astype(jnp.float32), w_head[member].astype(jnp.float32))
        err = ((pred - targets) * (2.0 / TOK)).astype(jnp.bfloat16)
        feats_split = feats.reshape(TICKS, feats.shape[1], N_DP, share, SW)
        err_split = err.reshape(TICKS, err.shape[1], N_DP, share, D)

        def add_share(total, index):
            own_feats = lax.dynamic_index_in_dim(feats_split, index, 2, keepdims=False).reshape(-1, SW)
            own_err = lax.dynamic_index_in_dim(err_split, index, 2, keepdims=False).reshape(-1, D)
            term = jnp.dot(own_feats.T, own_err, preferred_element_type=jnp.float32).astype(jnp.bfloat16)
            term = lax.optimization_barrier(term).astype(jnp.float32)
            return (total + term, None)
        total, _ = lax.scan(add_share, jnp.zeros((SW, D), jnp.float32), jnp.arange(N_DP).astype(jnp.int32))
        grads.append(total)
    return (advanced, jnp.stack(grads))
```

```python
import functools

import jax
import jax.numpy as jnp
from jax import lax
from jax.experimental import pallas as pl
from jax.experimental.pallas import tpu as pltpu
from jax.sharding import PartitionSpec as P

HEAD_SIZE = 128
LN_ROWS = 16
BF16 = jnp.bfloat16
F32 = jnp.float32
MESH = pl.DeviceIdType.MESH


def layer_norm(rows, gain):
    rows = rows.astype(F32)
    centred = rows - jnp.mean(rows, axis=-1, keepdims=True)
    spread = jnp.mean(centred * centred, axis=-1, keepdims=True)
    return centred * lax.rsqrt(spread + 1e-06) * gain


def attend(query, keys, values, same):
    scores = lax.dot_general(
        query, keys, (((1,), (1,)), ((), ())), preferred_element_type=F32
    ) * HEAD_SIZE ** (-0.5)
    scores = jnp.where(same, scores, -1e30)
    top = jnp.max(scores, axis=-1, keepdims=True)
    expo = jnp.exp(scores - top)
    probs = (expo / jnp.sum(expo, axis=-1, keepdims=True)).astype(BF16)
    return jnp.dot(probs, values, preferred_element_type=F32).astype(BF16)


def window_kernel(
    S, M, Z, T, pieces, turns,
    x_hbm, seg_ref, gain_ref, wqkv_ref, wout_ref, fgain_ref, srows_ref, sgain_ref, whead_ref,
    adv_ref, grad_ref,
    wqkv, wofull, whead, normed, xfull, mixfull, xs, xrows, fin, tg, tbuf, advbuf,
    sall, pred, fown, errs, x_ref, grad, det,
    local_sem, x_sem, out_sem, wo_s, wo_r, wf_s, wf_r, mx_s, mx_r, sh_s, sh_r, ar_s, ar_r, al_s, al_r,
    ro_s, ro_r, ad_s, ad_r, tg_s, tg_r, fe_s, fe_r, fp_s, fp_r,
    er_s, er_r, ml_s, ml_r, dz_s, dz_r, dx_s, dx_r,
):
    s = lax.axis_index("section")
    c = lax.axis_index("student")
    z = lax.axis_index("dp")
    root = S - 1
    tokens, model = x_ref.shape
    wid = wout_ref.shape[0]
    share = tokens // Z
    cw = model // Z
    block = whead_ref.shape[1]
    sw = whead_ref.shape[0]
    fw = sw // Z
    units = sw // 128
    other = max(1, units // (2 * S)) * 128
    first = sw - other * (S - 1)
    straight = tokens - det.shape[1]
    turn_rows = det.shape[1] // turns
    halves = 2 if M % 2 == 0 else 1
    part = c % halves
    hw = wid // halves
    sends = []

    def remote(src, dst, send, recv, where):
        return pltpu.make_async_remote_copy(
            src_ref=src, dst_ref=dst, send_sem=send, recv_sem=recv,
            device_id=where, device_id_type=MESH,
        )

    def post(cond, build):
        if cond is True:
            build().start()
        else:
            pl.when(cond)(lambda: build().start())
        sends.append((cond, build))

    def zmod(value):
        return lax.rem(value + Z, Z)

    def cols(index):
        return pl.ds(pl.multiple_of(index * cw, 128), cw)

    load_qkv = pltpu.make_async_copy(wqkv_ref, wqkv, local_sem.at[0])
    load_head = pltpu.make_async_copy(whead_ref, whead, local_sem.at[1])
    own_wo = pltpu.make_async_copy(
        wout_ref.at[:, cols(z)],
        wofull.at[pl.ds(pl.multiple_of(z * wid, wid), wid), :],
        local_sem.at[2],
    )
    xr = tokens // x_sem.shape[0]
    load_x = [
        pltpu.make_async_copy(
            x_hbm.at[pl.ds(i * xr, xr), :], x_ref.at[pl.ds(i * xr, xr), :], x_sem.at[i]
        )
        for i in range(x_sem.shape[0])
    ]
    load_rows = pltpu.make_async_copy(srows_ref, sall.at[0], local_sem.at[3])
    save_adv = pltpu.make_async_copy(advbuf, adv_ref, local_sem.at[4])

    barrier = pltpu.get_barrier_semaphore()

    def greet(where):
        pl.semaphore_signal(barrier, inc=1, device_id=where, device_id_type=MESH)

    for k in range(1, Z):
        greet((s, c, zmod(z + k)))
    for k in range(Z):
        pl.when(s > 0)(functools.partial(greet, (s - 1, c, zmod(z + k))))
        pl.when(s < root)(functools.partial(greet, (s + 1, c, zmod(z + k))))
    for at in range(S):
        far = jnp.logical_or(s - at > 1, at - s > 1)
        pl.when(far)(functools.partial(greet, (jnp.int32(at), c, z)))
        for dm in range(1, M):
            greet((jnp.int32(at), lax.rem(c + dm, M), z))
    for copy in load_x:
        copy.start()
    load_qkv.start()
    own_wo.start()
    load_rows.start()
    load_head.start()
    for at in range(S):
        near = min(at, 1) + min(root - at, 1)
        peers = (Z - 1) + Z * near + (S - 1 - near) + S * (M - 1)
        pl.when(s == at)(functools.partial(pl.semaphore_wait, barrier, peers))

    def wo_rows(source, which):
        return pl.ds(pl.multiple_of(source * wid + which * hw, hw), hw)

    for k in sorted(range(1, Z), reverse=True):
        def build(k=k):
            to = zmod(z + k)
            return remote(
                wout_ref.at[pl.ds(pl.multiple_of(part * hw, hw), hw), cols(to)],
                wofull.at[wo_rows(z, part), :],
                wo_s.at[k - 1], wo_r.at[k - 1], (s, c, to),
            )
        post(True, build)

    def pass_on(k):
        source = zmod(z - k)
        mine = wofull.at[wo_rows(source, part), :]
        mate = c + 1 - 2 * part
        return remote(mine, mine, wf_s.at[k - 1], wf_r.at[k - 1], (s, mate, z))

    def gather_wo():
        for k in range(1, Z):
            source = zmod(z - k)
            mine = wofull.at[wo_rows(source, part), :]
            remote(mine, mine, wo_s.at[k - 1], wo_r.at[k - 1], (s, c, source)).wait_recv()
            if halves == 2:
                post(True, functools.partial(pass_on, k))
        if halves == 2:
            for k in range(1, Z):
                source = zmod(z - k)
                other = wofull.at[wo_rows(source, 1 - part), :]
                remote(other, other, wf_s.at[k - 1], wf_r.at[k - 1],
                       (s, c + 1 - 2 * part, z)).wait_recv()
        own_wo.wait()

    def portion(index, zero):
        if zero:
            return pl.ds(0, first)
        return pl.ds(pl.multiple_of(first + (index - 1) * other, 128), other)

    def spread_rows(zero):
        cond = s == 0 if zero else s > 0
        for k in range(1, Z):
            def build(k=k):
                part = portion(s, zero)
                return remote(srows_ref.at[:, :, :, part], sall.at[k, :, :, :, part],
                              fe_s.at[k - 1], fe_r.at[k - 1], (s, c, zmod(z + k)))
            post(cond, build)

    def pass_rows(zero):
        def take():
            for k in range(1, Z):
                there = sall.at[k, :, :, :, portion(s, zero)]
                remote(there, there, fe_s.at[k - 1], fe_r.at[k - 1], (s, c, zmod(z - k))).wait_recv()
        cond = s == 0 if zero else s > 0
        pl.when(cond)(take)
        for k in range(1, S):
            def build(k=k):
                there = sall.at[pl.ds(1, Z - 1), :, :, :, portion(s, zero)]
                return remote(there, there, fp_s.at[k - 1], fp_r.at[k - 1],
                              (lax.rem(s + k, S), c, z))
            post(cond, build)

    def student():
        for k in range(1, S):
            where = lax.rem(s + S - k, S)

            def arrive(zero, k=k, where=where):
                there = sall.at[pl.ds(1, Z - 1), :, :, :, portion(where, zero)]
                remote(there, there, fp_s.at[k - 1], fp_r.at[k - 1], (where, c, z)).wait_recv()
            pl.when(where == 0)(functools.partial(arrive, True))
            pl.when(where > 0)(functools.partial(arrive, False))

        def one(k, carry):
            rows = layer_norm(sall[k].astype(F32).reshape(T * M * share, sw), sgain_ref[...])
            rows = rows.astype(BF16)
            for zz in range(Z):
                def own(zz=zz):
                    fown[k] = rows[:, zz * fw:(zz + 1) * fw].reshape(T, M * share, fw)
                pl.when(z == zz)(own)
            pred[k] = jnp.dot(rows, whead[...], preferred_element_type=F32).reshape(
                T, M, share, block
            )
            return carry

        lax.fori_loop(0, Z, one, 0)

    def spread(t, at_root):
        def take():
            there = tbuf.at[t, c, 0]
            remote(there, there, tg_s.at[t, 0], tg_r.at[t], (root, c, z)).wait_recv()
        if not at_root:
            pl.when(s != root)(take)
        for k in range(1, Z):
            def build(k=k):
                return remote(tbuf.at[t, c, 0], tbuf.at[t, c, k], er_s.at[t, k - 1],
                              er_r.at[t, k - 1], (s, c, zmod(z + k)))
            post(s == root if at_root else s != root, build)

    def relay(t):
        for k in range(Z):
            there = tbuf.at[t, c, k]
            if k:
                remote(there, there, er_s.at[t, k - 1], er_r.at[t, k - 1],
                       (s, c, zmod(z - k))).wait_recv()
            for dm in range(1, M):
                def build(k=k, dm=dm):
                    there = tbuf.at[t, c, k]
                    return remote(there, there, ml_s.at[t, dm - 1, k], ml_r.at[t, dm - 1, k],
                                  (s, lax.rem(c + dm, M), z))
                post(True, build)

    gw = block // out_sem.shape[0]

    def save_grad(j):
        at = pl.ds(j * gw, gw)
        return pltpu.make_async_copy(grad.at[:, at], grad_ref.at[:, at], out_sem.at[j])

    def gradient(t):
        for dm in range(1, M):
            for k in range(Z):
                who = lax.rem(c + M - dm, M)
                there = tbuf.at[t, who, k]
                remote(there, there, ml_s.at[t, dm - 1, k], ml_r.at[t, dm - 1, k],
                       (s, who, z)).wait_recv()

        def one(k, carry):
            err = (pred[k, t] - tbuf[t, :, k].astype(F32)) * (2.0 / tokens)
            errs[k] = err.reshape(M * share, block).astype(BF16)
            return carry

        lax.fori_loop(0, Z, one, 0)
        feats = fown[:, t].reshape(Z * M * share, fw)
        for j in range(block // gw):
            at = slice(j * gw, (j + 1) * gw)
            term = lax.dot_general(
                feats, errs[:, :, at].reshape(Z * M * share, gw),
                (((0,), (0,)), ((), ())), preferred_element_type=F32,
            )
            if t == 0:
                grad[:, at] = term
            else:
                grad[:, at] += term
            if t == T - 1:
                save_grad(j).start()

    def turned(t):
        return root - (T - 1) + t

    def forward(t):
        cond = jnp.logical_and(s >= t, s + 1 <= turned(t + 1))
        for r in range(turns):
            at = pl.ds(r * turn_rows, turn_rows)

            def take(r=r, at=at):
                for k in range(1, Z):
                    there = det.at[t, at, cols(zmod(z - k))]
                    remote(there, there, dz_s.at[t, k - 1, r], dz_r.at[t, k - 1, r],
                           (s, c, zmod(z - k))).wait_recv()

            def build(r=r, at=at):
                return remote(det.at[t, at, :],
                              xfull.at[t, pl.ds(straight + r * turn_rows, turn_rows), :],
                              dx_s.at[t, r], dx_r.at[t, r], (s + 1, c, z))
            pl.when(cond)(take)
            post(cond, build)

    def gather_state(t, active):
        all_straight = turned(t) < root

        def piece(r, origin):
            low, size = pieces[r]
            return xfull.at[t - 1, pl.ds(low, size), cols(origin)]

        def used(r):
            if pieces[r][0] < straight:
                return active
            return jnp.logical_and(active, s > turned(t))

        numbers = [r for r in range(len(pieces)) if pieces[r][0] < straight or all_straight]

        def to_right(r, k):
            there = piece(r, z - k)
            return remote(there, there, ar_s.at[t - 1, k, r], ar_r.at[t - 1, k, r], (s, c, z + 1))

        def to_left(r, k):
            there = piece(r, z + k)
            return remote(there, there, al_s.at[t - 1, k, r], al_r.at[t - 1, k, r], (s, c, z - 1))

        def right_from(r, k):
            there = piece(r, z - k)
            remote(there, there, ar_s.at[t - 1, k - 1, r], ar_r.at[t - 1, k - 1, r],
                   (s, c, z - 1)).wait_recv()

        def left_from(r, k):
            there = piece(r, z + k)
            remote(there, there, al_s.at[t - 1, k - 1, r], al_r.at[t - 1, k - 1, r],
                   (s, c, z + 1)).wait_recv()

        if t > 1:
            forward(t - 1)
        for r in numbers:
            def first(r=r):
                there = piece(r, z)
                remote(there, there, sh_s.at[t - 1, r], sh_r.at[t - 1, r],
                       (s - 1, c, z)).wait_recv()
            pl.when(used(r))(first)
            post(jnp.logical_and(used(r), z < Z - 1), functools.partial(to_right, r, 0))
            post(jnp.logical_and(used(r), z > 0), functools.partial(to_left, r, 0))
        if t == 1:
            forward(0)
        for k in range(1, Z):
            for r in numbers:
                pl.when(jnp.logical_and(used(r), z >= k))(functools.partial(right_from, r, k))
                if k < Z - 1:
                    post(jnp.logical_and(used(r), jnp.logical_and(z >= k, z < Z - 1)),
                         functools.partial(to_right, r, k))
                pl.when(jnp.logical_and(used(r), z + k < Z))(functools.partial(left_from, r, k))
                if k < Z - 1:
                    post(jnp.logical_and(used(r), jnp.logical_and(z + k < Z, z > 0)),
                         functools.partial(to_left, r, k))

        def landed():
            for r in range(turns):
                there = xfull.at[t - 1, pl.ds(straight + r * turn_rows, turn_rows), :]
                remote(there, there, dx_s.at[t - 1, r], dx_r.at[t - 1, r],
                       (s - 1, c, z)).wait_recv()
        pl.when(jnp.logical_and(active, s <= turned(t)))(landed)

    def mix_cols(index):
        return pl.ds(pl.multiple_of(index * wid, 128), wid)

    def mixing(t):
        source = x_ref if t == 0 else xfull.at[t - 1]
        if t == 0:
            for copy in load_x:
                copy.wait()

        def norm_rows(i, carry):
            rows = pl.ds(pl.multiple_of(i * LN_ROWS, LN_ROWS), LN_ROWS)
            normed[rows, :] = layer_norm(source[rows, :], gain_ref[...]).astype(BF16)
            return carry

        lax.fori_loop(0, tokens // LN_ROWS, norm_rows, 0)
        if t == 0:
            load_qkv.wait()
        rows = normed[...]
        query, keys, values = [
            jnp.dot(rows, wqkv[j], preferred_element_type=F32).astype(BF16)
            for j in range(3)
        ]
        crops = jnp.broadcast_to(seg_ref[s - t].astype(F32), (tokens, tokens))
        same = crops == crops.T
        outs = []
        for h in range(wid // HEAD_SIZE):
            at = slice(h * HEAD_SIZE, (h + 1) * HEAD_SIZE)
            outs.append(attend(query[:, at], keys[:, at], values[:, at], same))
        mixfull[t, :, mix_cols(z)] = jnp.concatenate(outs, axis=1)

    def send_mixed(t, active):
        for k in range(1, Z):
            def build(k=k):
                own = mixfull.at[t, :, mix_cols(z)]
                return remote(own, own, mx_s.at[t, k - 1], mx_r.at[t, k - 1],
                              (s, c, zmod(z + k)))
            post(active, build)

    def project(t):
        for k in range(1, Z):
            there = mixfull.at[t, :, mix_cols(zmod(z - k))]
            remote(there, there, mx_s.at[t, k - 1], mx_r.at[t, k - 1],
                   (s, c, zmod(z - k))).wait_recv()
        own = x_ref[:, cols(z)] if t == 0 else xfull[t - 1, :, cols(z)]
        summed = own.astype(F32) + jnp.dot(mixfull[t], wofull[...], preferred_element_type=F32)
        if t < T - 1:
            xs[t] = summed.astype(BF16)
            det[t, :, cols(z)] = summed[straight:].astype(BF16)
        xrows[t] = summed.reshape(Z, share, cw).astype(BF16)

    def send_state(t, active):
        if t < T - 1:
            go = jnp.logical_and(active, s < root)
            bend = jnp.logical_and(go, s + 1 <= turned(t + 1))
            for r in range(turns):
                for k in range(1, Z):
                    def build_turn(r=r, k=k):
                        there = det.at[t, pl.ds(r * turn_rows, turn_rows), cols(z)]
                        return remote(there, there, dz_s.at[t, k - 1, r], dz_r.at[t, k - 1, r],
                                      (s, c, zmod(z + k)))
                    post(bend, build_turn)
            for r, (low, size) in enumerate(pieces):
                def build(r=r, low=low, size=size):
                    at = pl.ds(low, size)
                    return remote(xs.at[t, at, :], xfull.at[t, at, cols(z)],
                                  sh_s.at[t, r], sh_r.at[t, r], (s + 1, c, z))
                if low < straight:
                    post(go, build)
                elif turned(t + 1) < root:
                    post(jnp.logical_and(go, s + 1 > turned(t + 1)), build)
        else:
            for k in range(Z):
                def build(k=k):
                    to = zmod(z + k)
                    return remote(xrows.at[t, to], advbuf.at[:, cols(z)],
                                  ad_s.at[k], ad_r.at[k], (s + 1, c, to))
                post(jnp.logical_and(active, s < root), build)
        for k in range(1, Z):
            def build_row(k=k):
                to = zmod(z + k)
                return remote(xrows.at[t, to], fin.at[t, :, cols(z)],
                              ro_s.at[t, k - 1], ro_r.at[t, k - 1], (s, c, to))
            post(s == root, build_row)

    def finish(t):
        def rows():
            fin[t, :, cols(z)] = xrows[t, z]
            for k in range(1, Z):
                there = fin.at[t, :, cols(zmod(z - k))]
                remote(there, there, ro_s.at[t, k - 1], ro_r.at[t, k - 1],
                       (s, c, zmod(z - k))).wait_recv()
            tg[t] = layer_norm(fin[t], fgain_ref[...]).astype(BF16)
            tbuf[t, c, 0] = tg[t, :, root * block:(root + 1) * block]

        pl.when(s == root)(rows)
        for to in range(root):
            def build(to=to):
                return remote(tg.at[t, :, to * block:(to + 1) * block], tbuf.at[t, c, 0],
                              tg_s.at[t, to], tg_r.at[t], (jnp.int32(to), c, z))
            post(s == root, build)

    def nothing():
        advbuf[...] = jnp.zeros_like(advbuf)
        save_adv.start()

    for t in range(T):
        active = True if t == 0 else s >= t
        if t == 0:
            mixing(0)
        else:
            gather_state(t, active)
            finish(t - 1)
            spread(t - 1, True)
            if t == 1:
                spread_rows(False)
            pl.when(active)(functools.partial(mixing, t))
        send_mixed(t, active)
        if t == 0:
            pl.when(s < T)(nothing)
            gather_wo()
            project(0)
        else:
            if t == T - 1:
                for before in range(1, t):
                    spread(before, False)
                load_head.wait()
                pl.when(s != root)(student)
                for before in range(t):
                    relay(before)
            pl.when(active)(functools.partial(project, t))
        send_state(t, active)
        if t == 0:
            load_rows.wait()
            spread_rows(True)
        elif t == 1:
            if t < T - 1:
                spread(0, False)
            pass_rows(True)
            pass_rows(False)

    finish(T - 1)
    spread(T - 1, True)
    pl.when(s == root)(student)
    for before in range(T - 1):
        gradient(before)
    spread(T - 1, False)
    relay(T - 1)
    gradient(T - 1)

    def arrived():
        for k in range(Z):
            there = advbuf.at[:, cols(zmod(z - k))]
            remote(there, there, ad_s.at[k], ad_r.at[k], (s - 1, c, zmod(z - k))).wait_recv()
        save_adv.start()

    pl.when(s >= T)(arrived)
    save_adv.wait()
    for j in range(block // gw):
        save_grad(j).wait()
    for cond, build in sends:
        if cond is True:
            build().wait_send()
        else:
            pl.when(cond)(lambda build=build: build().wait_send())


def solution(mesh):
    S, M, Z = mesh.shape["section"], mesh.shape["student"], mesh.shape["dp"]

    def on_device(
        in_flight, segments, norm_gain, w_qkv, w_out, final_gain, student_rows, student_gain, w_head
    ):
        tokens, model = in_flight.shape[2:]
        wid = w_out.shape[1]
        T, share = student_rows.shape[1], tokens // Z
        sw, block = w_head.shape[1:]
        cw, fw = model // Z, sw // Z
        grain = tokens // 8
        straight, turns = 5 * grain, 3
        pieces = ((0, 2 * grain), (2 * grain, 2 * grain), (4 * grain, grain), (straight, 3 * grain))
        R = len(pieces)
        vmem = pl.BlockSpec(memory_space=pltpu.VMEM)
        hbm = pl.BlockSpec(memory_space=pl.ANY)
        dma = pltpu.SemaphoreType.DMA
        K = max(Z - 1, 1)
        adv, grad = pl.pallas_call(
            functools.partial(window_kernel, S, M, Z, T, pieces, turns),
            out_shape=(
                jax.ShapeDtypeStruct((share, model), BF16),
                jax.ShapeDtypeStruct((fw, block), F32),
            ),
            in_specs=[hbm, vmem, vmem, hbm, hbm, vmem, hbm, vmem, hbm],
            out_specs=(hbm, hbm),
            scratch_shapes=[
                pltpu.VMEM((3, model, wid), BF16),
                pltpu.VMEM((Z * wid, cw), BF16),
                pltpu.VMEM((sw, block), BF16),
                pltpu.VMEM((tokens, model), BF16),
                pltpu.VMEM((T - 1, tokens, model), BF16),
                pltpu.VMEM((T, tokens, Z * wid), BF16),
                pltpu.VMEM((T - 1, tokens, cw), BF16),
                pltpu.VMEM((T, Z, share, cw), BF16),
                pltpu.VMEM((T, share, model), BF16),
                pltpu.VMEM((T, share, model), BF16),
                pltpu.VMEM((T, M, Z, share, block), BF16),
                pltpu.VMEM((share, model), BF16),
                pltpu.VMEM((Z, T, M, share, sw), BF16),
                pltpu.VMEM((Z, T, M, share, block), F32),
                pltpu.VMEM((Z, T, M * share, fw), BF16),
                pltpu.VMEM((Z, M * share, block), BF16),
                pltpu.VMEM((tokens, model), BF16),
                pltpu.VMEM((fw, block), F32),
                pltpu.VMEM((T - 1, tokens - straight, model), BF16),
                dma((5,)), dma((4,)), dma((4 if block % 512 == 0 else 1,)),
                dma((K,)), dma((K,)), dma((K,)), dma((K,)),
                dma((T, K)), dma((T, K)),
                dma((T - 1, R)), dma((T - 1, R)),
                dma((T - 1, K, R)), dma((T - 1, K, R)),
                dma((T - 1, K, R)), dma((T - 1, K, R)),
                dma((T, K)), dma((T, K)),
                dma((Z,)), dma((Z,)),
                dma((T, S)), dma((T,)),
                dma((K,)), dma((K,)), dma((S,)), dma((S,)),
                dma((T, K)), dma((T, K)),
                dma((T, M, Z)), dma((T, M, Z)),
                dma((T - 1, K, turns)), dma((T - 1, K, turns)), dma((T - 1, turns)), dma((T - 1, turns)),
            ],
            compiler_params=pltpu.CompilerParams(
                collective_id=0, has_side_effects=True, vmem_limit_bytes=58 << 20
            ),
        )(
            in_flight[0, 0], segments, norm_gain, jnp.transpose(w_qkv[0], (1, 0, 2)), w_out[0],
            final_gain[None], student_rows[0], student_gain, w_head[0],
        )
        return adv[None, None], grad[None]

    in_specs = (
        P("section", "student", None, None),
        P(None, "student", None),
        P("section", None),
        P("section", None, None, "dp"),
        P("section", "dp", None),
        P(),
        P("student", None, None, "dp", None),
        P("student", None),
        P("student", None, "section"),
    )
    out_specs = (P("section", "student", "dp", None), P("student", "dp", "section"))
    return jax.shard_map(
        on_device, mesh=mesh, in_specs=in_specs, out_specs=out_specs, check_vma=False
    )
```

```python
import functools

import jax
import jax.numpy as jnp
from jax import lax
from jax.experimental import pallas as pl
from jax.experimental.pallas import tpu as pltpu
from jax.sharding import PartitionSpec as P

HEAD_SIZE = 128
LN_ROWS = 16
BF16 = jnp.bfloat16
F32 = jnp.float32
MESH = pl.DeviceIdType.MESH


def layer_norm(rows, gain):
    rows = rows.astype(F32)
    centred = rows - jnp.mean(rows, axis=-1, keepdims=True)
    spread = jnp.mean(centred * centred, axis=-1, keepdims=True)
    return centred * lax.rsqrt(spread + 1e-06) * gain


def attend(query, keys, values, same):
    scores = lax.dot_general(
        query, keys, (((1,), (1,)), ((), ())), preferred_element_type=F32
    ) * HEAD_SIZE ** (-0.5)
    scores = jnp.where(same, scores, -1e30)
    top = jnp.max(scores, axis=-1, keepdims=True)
    expo = jnp.exp(scores - top)
    probs = (expo / jnp.sum(expo, axis=-1, keepdims=True)).astype(BF16)
    return jnp.dot(probs, values, preferred_element_type=F32).astype(BF16)


def window_kernel(
    S, M, Z, T, pieces, turns,
    x_hbm, seg_ref, gain_ref, wqkv_ref, wout_ref, fgain_ref, srows_ref, sgain_ref, whead_ref,
    adv_ref, grad_ref,
    wqkv, wofull, whead, normed, xfull, mixfull, xs, xrows, fin, tg, tbuf, advbuf,
    sall, pred, fown, errs, x_ref, grad, det,
    local_sem, x_sem, out_sem, wo_s, wo_r, wf_s, wf_r, mx_s, mx_r, sh_s, sh_r, ar_s, ar_r, al_s, al_r,
    ro_s, ro_r, ad_s, ad_r, tg_s, tg_r, fe_s, fe_r, fp_s, fp_r,
    er_s, er_r, ml_s, ml_r, dz_s, dz_r, dx_s, dx_r,
):
    s = lax.axis_index("section")
    c = lax.axis_index("student")
    z = lax.axis_index("dp")
    root = S - 1
    tokens, model = x_ref.shape
    wid = wout_ref.shape[0]
    share = tokens // Z
    cw = model // Z
    block = whead_ref.shape[1]
    sw = whead_ref.shape[0]
    fw = sw // Z
    straight = tokens - det.shape[1]
    turn_rows = det.shape[1] // turns
    halves = 2 if M % 2 == 0 else 1
    part = c % halves
    hw = wid // halves
    sends = []
    owners = tuple(t if t < T - 1 and t < root else root for t in range(T))

    def remote(src, dst, send, recv, where):
        return pltpu.make_async_remote_copy(
            src_ref=src, dst_ref=dst, send_sem=send, recv_sem=recv,
            device_id=where, device_id_type=MESH,
        )

    def go(cond, build):
        if cond is True:
            build().start()
        else:
            pl.when(cond)(lambda: build().start())

    def owe(cond, ref, sem):
        sends.append((cond, lambda: remote(ref, ref, sem, sem, (s, c, zmod(z + 1)))))

    def landed(ref, sem):
        remote(ref, ref, sem, sem, (s, c, zmod(z + 1))).wait_recv()

    def post(cond, build):
        go(cond, build)
        sends.append((cond, build))

    def zmod(value):
        return lax.rem(value + Z, Z)

    def cols(index):
        return pl.ds(pl.multiple_of(index * cw, 128), cw)

    load_qkv = pltpu.make_async_copy(wqkv_ref, wqkv, local_sem.at[0])
    load_head = pltpu.make_async_copy(whead_ref, whead, local_sem.at[1])
    own_wo = pltpu.make_async_copy(
        wout_ref.at[:, cols(z)],
        wofull.at[pl.ds(pl.multiple_of(z * wid, wid), wid), :],
        local_sem.at[2],
    )
    xr = tokens // x_sem.shape[0]
    load_x = [
        pltpu.make_async_copy(
            x_hbm.at[pl.ds(i * xr, xr), :], x_ref.at[pl.ds(i * xr, xr), :], x_sem.at[i]
        )
        for i in range(x_sem.shape[0])
    ]
    load_rows = pltpu.make_async_copy(srows_ref, sall.at[0], local_sem.at[3])
    save_adv = pltpu.make_async_copy(advbuf, adv_ref, local_sem.at[4])

    barrier = pltpu.get_barrier_semaphore()

    def greet(where):
        pl.semaphore_signal(barrier, inc=1, device_id=where, device_id_type=MESH)

    for at in range(S):
        for k in range(Z):
            if k:
                greet((jnp.int32(at), c, zmod(z + k)))
            else:
                pl.when(s != at)(functools.partial(greet, (jnp.int32(at), c, z)))
        for dm in range(1, M):
            greet((jnp.int32(at), lax.rem(c + dm, M), z))
    for copy in load_x:
        copy.start()
    load_qkv.start()
    own_wo.start()
    load_rows.start()
    load_head.start()
    pl.semaphore_wait(barrier, S * Z - 1 + S * (M - 1))

    def wo_rows(source, which):
        return pl.ds(pl.multiple_of(source * wid + which * hw, hw), hw)

    for k in sorted(range(1, Z), reverse=True):
        def build(k=k):
            to = zmod(z + k)
            return remote(
                wout_ref.at[pl.ds(pl.multiple_of(part * hw, hw), hw), cols(to)],
                wofull.at[wo_rows(z, part), :],
                wo_s.at[0], wo_r.at[k - 1], (s, c, to),
            )
        go(True, build)
    owe(True, wofull.at[pl.ds(0, (Z - 1) * hw), :], wo_s.at[0])

    def pass_on(k):
        source = zmod(z - k)
        mine = wofull.at[wo_rows(source, part), :]
        mate = c + 1 - 2 * part
        return remote(mine, mine, wf_s.at[0], wf_r.at[k - 1], (s, mate, z))

    def gather_wo():
        for k in range(1, Z):
            source = zmod(z - k)
            mine = wofull.at[wo_rows(source, part), :]
            landed(mine, wo_r.at[k - 1])
            if halves == 2:
                go(True, functools.partial(pass_on, k))
        if halves == 2:
            owe(True, wofull.at[pl.ds(0, (Z - 1) * hw), :], wf_s.at[0])
            for k in range(1, Z):
                source = zmod(z - k)
                other = wofull.at[wo_rows(source, 1 - part), :]
                landed(other, wf_r.at[k - 1])
        own_wo.wait()

    def spread_rows():
        for k in range(1, Z):
            def build(k=k):
                return remote(srows_ref, sall.at[k], fe_s.at[0], fe_r.at[k - 1],
                              (s, c, zmod(z + k)))
            go(s == 0, build)
        owe(s == 0, sall.at[pl.ds(0, Z - 1)], fe_s.at[0])

    handed = (1,) if root > 1 else ()

    def pass_rows():
        for k in range(1, Z):
            pl.when(s == 0)(functools.partial(landed, sall.at[k], fe_r.at[k - 1]))
            for to in range(S - 1, 0, -1):
                def build(k=k, to=to):
                    there = sall.at[k]
                    return remote(there, there, fp_s.at[k - 1, to - 1], fp_r.at[k - 1],
                                  (jnp.int32(to), c, z))
                if to != root or k not in handed:
                    post(s == 0, build)

    def hand_rows():
        for k in handed:
            there = sall.at[k]

            def build(k=k, there=there):
                return remote(there, there, fp_s.at[k - 1, root - 1], fp_r.at[k - 1],
                              (jnp.int32(root), c, z))
            pl.when(s == 1)(functools.partial(landed, there, fp_r.at[k - 1]))
            post(s == 1, build)

    def student():
        for k in range(1, Z):
            pl.when(s > 1 if k in handed else s > 0)(
                functools.partial(landed, sall.at[k], fp_r.at[k - 1])
            )

        def one(k, carry):
            rows = layer_norm(sall[k].astype(F32).reshape(T * M * share, sw), sgain_ref[...])
            rows = rows.astype(BF16)
            for zz in range(Z):
                def own(zz=zz):
                    fown[k] = rows[:, zz * fw:(zz + 1) * fw].reshape(T, M * share, fw)
                pl.when(z == zz)(own)
            pred[k] = jnp.dot(rows, whead[...], preferred_element_type=F32).reshape(
                T, M, share, block
            )
            return carry

        lax.fori_loop(0, Z, one, 0)

    def spread(t, who):
        pl.when(jnp.logical_and(who, s != owners[t]))(
            functools.partial(landed, tbuf.at[t, c, 0], tg_r.at[t])
        )
        for k in range(1, Z):
            def build(k=k):
                return remote(tbuf.at[t, c, 0], tbuf.at[t, c, k], er_s.at[t],
                              er_r.at[t, k - 1], (s, c, zmod(z + k)))
            go(who, build)
        owe(who, tbuf.at[t, c, pl.ds(0, Z - 1)], er_s.at[t])

    def relay(t):
        for k in range(Z):
            there = tbuf.at[t, c, k]
            if k:
                landed(there, er_r.at[t, k - 1])
            for dm in range(1, M):
                def build(k=k, dm=dm):
                    there = tbuf.at[t, c, k]
                    return remote(there, there, ml_s.at[t], ml_r.at[t, dm - 1],
                                  (s, lax.rem(c + dm, M), z))
                go(True, build)
        if M > 1:
            owe(True, tbuf.at[t, pl.ds(0, M - 1)], ml_s.at[t])

    gw = block // out_sem.shape[0]

    def save_grad(j):
        at = pl.ds(j * gw, gw)
        return pltpu.make_async_copy(grad.at[:, at], grad_ref.at[:, at], out_sem.at[j])

    def gradient(t):
        for dm in range(1, M):
            landed(tbuf.at[t, lax.rem(c + M - dm, M)], ml_r.at[t, dm - 1])

        def one(k, carry):
            err = (pred[k, t] - tbuf[t, :, k].astype(F32)) * (2.0 / tokens)
            errs[k] = err.reshape(M * share, block).astype(BF16)
            return carry

        lax.fori_loop(0, Z, one, 0)
        feats = fown[:, t].reshape(Z * M * share, fw)
        for j in range(block // gw):
            at = slice(j * gw, (j + 1) * gw)
            term = lax.dot_general(
                feats, errs[:, :, at].reshape(Z * M * share, gw),
                (((0,), (0,)), ((), ())), preferred_element_type=F32,
            )
            if t == 0:
                grad[:, at] = term
            else:
                grad[:, at] += term
            if t == T - 1:
                save_grad(j).start()

    def turned(t):
        return root - (T - 1) + t

    def forward(t):
        cond = jnp.logical_and(s >= t, s + 1 <= turned(t + 1))
        for r in range(turns):
            at = pl.ds(r * turn_rows, turn_rows)

            def build(r=r, at=at):
                return remote(det.at[t, at, :],
                              xfull.at[t, pl.ds(straight + r * turn_rows, turn_rows), :],
                              dx_s.at[t], dx_r.at[t, r], (s + 1, c, z))
            whole = det.at[t, at, pl.ds(0, (Z - 1) * cw)]
            pl.when(cond)(functools.partial(landed, whole, dz_r.at[t, r]))
            go(cond, build)
        owe(cond, det.at[t], dx_s.at[t])

    def gather_state(t, active):
        all_straight = turned(t) < root

        def piece(r, origin):
            low, size = pieces[r]
            return xfull.at[t - 1, pl.ds(low, size), cols(origin)]

        def used(r):
            if pieces[r][0] < straight:
                return active
            return jnp.logical_and(active, s > turned(t))

        numbers = [r for r in range(len(pieces)) if pieces[r][0] < straight or all_straight]

        def to_right(r, k):
            there = piece(r, z - k)
            return remote(there, there, ar_s.at[t - 1, k, part_of(r)], ar_r.at[t - 1, k, r],
                          (s, c, z + 1))

        def to_left(r, k):
            there = piece(r, z + k)
            return remote(there, there, al_s.at[t - 1, k, part_of(r)], al_r.at[t - 1, k, r],
                          (s, c, z - 1))

        def part_of(r):
            return 0 if pieces[r][0] < straight else 1

        def send(cond, build, r, k, sem):
            go(jnp.logical_and(used(r), cond), functools.partial(build, r, k))
            size = straight if r == 0 else tokens - straight
            if r == 0 or part_of(r):
                owe(jnp.logical_and(used(r), cond),
                    xfull.at[t - 1, pl.ds(0, size), pl.ds(0, cw)], sem.at[t - 1, k, part_of(r)])

        for r in numbers:
            pl.when(used(r))(functools.partial(landed, piece(r, z), sh_r.at[t - 1, r]))
            send(z < Z - 1, to_right, r, 0, ar_s)
            send(z > 0, to_left, r, 0, al_s)
        if t == 1:
            forward(0)
        for k in range(1, Z):
            for r in numbers:
                pl.when(jnp.logical_and(used(r), z >= k))(
                    functools.partial(landed, piece(r, z - k), ar_r.at[t - 1, k - 1, r])
                )
                if k < Z - 1:
                    send(jnp.logical_and(z >= k, z < Z - 1), to_right, r, k, ar_s)
                pl.when(jnp.logical_and(used(r), z + k < Z))(
                    functools.partial(landed, piece(r, z + k), al_r.at[t - 1, k - 1, r])
                )
                if k < Z - 1:
                    send(jnp.logical_and(z + k < Z, z > 0), to_left, r, k, al_s)

        def turned_in():
            for r in range(turns):
                landed(xfull.at[t - 1, pl.ds(straight + r * turn_rows, turn_rows), :],
                       dx_r.at[t - 1, r])
        pl.when(jnp.logical_and(active, s <= turned(t)))(turned_in)

    def mix_cols(index):
        return pl.ds(pl.multiple_of(index * wid, 128), wid)

    def mixing(t):
        source = x_ref if t == 0 else xfull.at[t - 1]
        if t == 0:
            for copy in load_x:
                copy.wait()

        def norm_rows(i, carry):
            rows = pl.ds(pl.multiple_of(i * LN_ROWS, LN_ROWS), LN_ROWS)
            normed[rows, :] = layer_norm(source[rows, :], gain_ref[...]).astype(BF16)
            return carry

        lax.fori_loop(0, tokens // LN_ROWS, norm_rows, 0)
        if t == 0:
            load_qkv.wait()
        rows = normed[...]
        query, keys, values = [
            jnp.dot(rows, wqkv[j], preferred_element_type=F32).astype(BF16)
            for j in range(3)
        ]
        crops = jnp.broadcast_to(seg_ref[s - t].astype(F32), (tokens, tokens))
        same = crops == crops.T
        outs = []
        for h in range(wid // HEAD_SIZE):
            at = slice(h * HEAD_SIZE, (h + 1) * HEAD_SIZE)
            outs.append(attend(query[:, at], keys[:, at], values[:, at], same))
        mixfull[t, :, mix_cols(z)] = jnp.concatenate(outs, axis=1)

    def send_mixed(t, active):
        for k in range(1, Z):
            def build(k=k):
                own = mixfull.at[t, :, mix_cols(z)]
                return remote(own, own, mx_s.at[t], mx_r.at[t], (s, c, zmod(z + k)))
            go(active, build)
        owe(active, mixfull.at[t, :, pl.ds(0, (Z - 1) * wid)], mx_s.at[t])

    def project(t):
        landed(mixfull.at[t, :, pl.ds(0, (Z - 1) * wid)], mx_r.at[t])
        own = x_ref[:, cols(z)] if t == 0 else xfull[t - 1, :, cols(z)]
        summed = own.astype(F32) + jnp.dot(mixfull[t], wofull[...], preferred_element_type=F32)
        if t < T - 1:
            xs[t] = summed.astype(BF16)
            det[t, :, cols(z)] = summed[straight:].astype(BF16)
        xrows[t] = summed.reshape(Z, share, cw).astype(BF16)

    def send_state(t, active):
        if t < T - 1:
            go_on = jnp.logical_and(active, s < root)
            bend = jnp.logical_and(go_on, s + 1 <= turned(t + 1))
            for r in range(turns):
                for k in range(1, Z):
                    def build_turn(r=r, k=k):
                        there = det.at[t, pl.ds(r * turn_rows, turn_rows), cols(z)]
                        return remote(there, there, dz_s.at[t], dz_r.at[t, r],
                                      (s, c, zmod(z + k)))
                    go(bend, build_turn)
            owe(bend, det.at[t, :, pl.ds(0, (Z - 1) * cw)], dz_s.at[t])
            for r, (low, size) in enumerate(pieces):
                def build(r=r, low=low, size=size):
                    at = pl.ds(low, size)
                    return remote(xs.at[t, at, :], xfull.at[t, at, cols(z)],
                                  sh_s.at[t, 0 if low < straight else 1], sh_r.at[t, r],
                                  (s + 1, c, z))
                if low < straight:
                    go(go_on, build)
                elif turned(t + 1) < root:
                    post(jnp.logical_and(go_on, s + 1 > turned(t + 1)), build)
            owe(go_on, xs.at[t, pl.ds(0, straight), :], sh_s.at[t, 0])
        else:
            for k in range(Z):
                def build(k=k):
                    to = zmod(z + k)
                    return remote(xrows.at[t, to], advbuf.at[:, cols(z)],
                                  ad_s.at[0], ad_r.at[0], (s + 1, c, to))
                go(jnp.logical_and(active, s < root), build)
            owe(jnp.logical_and(active, s < root), advbuf, ad_s.at[0])
        low = 0 if owners[t] != root else 1
        for k in range(low, Z):
            def build_row(k=k):
                to = zmod(z + k)
                return remote(xrows.at[t, to], fin.at[t, :, cols(z)],
                              ro_s.at[t], ro_r.at[t], (jnp.int32(owners[t]), c, to))
            go(s == root, build_row)
        owe(s == root, fin.at[t, :, pl.ds(0, (Z - low) * cw)], ro_s.at[t])

    def finish(t):
        own = owners[t]

        def rows():
            if own == root:
                fin[t, :, cols(z)] = xrows[t, z]
            landed(fin.at[t, :, pl.ds(0, (Z - (own == root)) * cw)], ro_r.at[t])
            tg[t] = layer_norm(fin[t], fgain_ref[...]).astype(BF16)
            tbuf[t, c, 0] = tg[t, :, own * block:(own + 1) * block]

        pl.when(s == own)(rows)
        for to in range(S):
            if to != own:
                def build(to=to):
                    return remote(tg.at[t, :, to * block:(to + 1) * block], tbuf.at[t, c, 0],
                                  tg_s.at[t], tg_r.at[t], (jnp.int32(to), c, z))
                go(s == own, build)
        owe(s == own, tg.at[t, :, pl.ds(0, (S - 1) * block)], tg_s.at[t])

    def nothing():
        advbuf[...] = jnp.zeros_like(advbuf)
        save_adv.start()

    last, others = s == root, s != root
    for t in range(T):
        active = True if t == 0 else s >= t
        if t == 0:
            mixing(0)
        elif t == 1:
            finish(0)
            gather_state(1, active)
            spread_rows()
            pass_rows()
            spread(0, last)
            pl.when(active)(functools.partial(mixing, t))
        else:
            if t == T - 1:
                hand_rows()
            forward(t - 1)
            gather_state(t, jnp.logical_and(active, others))
            pl.when(active)(functools.partial(mixing, t))
        send_mixed(t, active)
        if t == 0:
            pl.when(s < T)(nothing)
            gather_wo()
            project(0)
        else:
            if t < T - 1:
                gather_state(t + 1, last)
            else:
                load_head.wait()
                for before in range(1, t):
                    finish(before)
                    spread(before, others)
                relay(0)
            pl.when(active)(functools.partial(project, t))
        send_state(t, active)
        if t == 0:
            load_rows.wait()
        elif t == 1:
            spread(0, others)

    finish(T - 1)
    spread(T - 1, last)
    for before in range(1, T - 1):
        spread(before, last)
    spread(T - 1, others)
    student()
    for before in range(1, T - 1):
        relay(before)
    for before in range(T - 1):
        gradient(before)
    relay(T - 1)
    gradient(T - 1)

    def arrived():
        landed(advbuf, ad_r.at[0])
        save_adv.start()

    pl.when(s >= T)(arrived)
    save_adv.wait()
    for j in range(block // gw):
        save_grad(j).wait()
    for cond, build in sends:
        if cond is True:
            build().wait_send()
        else:
            pl.when(cond)(lambda build=build: build().wait_send())


def solution(mesh):
    S, M, Z = mesh.shape["section"], mesh.shape["student"], mesh.shape["dp"]

    def on_device(
        in_flight, segments, norm_gain, w_qkv, w_out, final_gain, student_rows, student_gain, w_head
    ):
        tokens, model = in_flight.shape[2:]
        wid = w_out.shape[1]
        T, share = student_rows.shape[1], tokens // Z
        sw, block = w_head.shape[1:]
        cw, fw = model // Z, sw // Z
        grain = tokens // 8
        straight, turns = 5 * grain, 3
        pieces = ((0, 2 * grain), (2 * grain, 2 * grain), (4 * grain, grain), (straight, 3 * grain))
        R = len(pieces)
        vmem = pl.BlockSpec(memory_space=pltpu.VMEM)
        hbm = pl.BlockSpec(memory_space=pl.ANY)
        dma = pltpu.SemaphoreType.DMA
        K = max(Z - 1, 1)
        adv, grad = pl.pallas_call(
            functools.partial(window_kernel, S, M, Z, T, pieces, turns),
            out_shape=(
                jax.ShapeDtypeStruct((share, model), BF16),
                jax.ShapeDtypeStruct((fw, block), F32),
            ),
            in_specs=[hbm, vmem, vmem, hbm, hbm, vmem, hbm, vmem, hbm],
            out_specs=(hbm, hbm),
            scratch_shapes=[
                pltpu.VMEM((3, model, wid), BF16),
                pltpu.VMEM((Z * wid, cw), BF16),
                pltpu.VMEM((sw, block), BF16),
                pltpu.VMEM((tokens, model), BF16),
                pltpu.VMEM((T - 1, tokens, model), BF16),
                pltpu.VMEM((T, tokens, Z * wid), BF16),
                pltpu.VMEM((T - 1, tokens, cw), BF16),
                pltpu.VMEM((T, Z, share, cw), BF16),
                pltpu.VMEM((T, share, model), BF16),
                pltpu.VMEM((T, share, model), BF16),
                pltpu.VMEM((T, M, Z, share, block), BF16),
                pltpu.VMEM((share, model), BF16),
                pltpu.VMEM((Z, T, M, share, sw), BF16),
                pltpu.VMEM((Z, T, M, share, block), F32),
                pltpu.VMEM((Z, T, M * share, fw), BF16),
                pltpu.VMEM((Z, M * share, block), BF16),
                pltpu.VMEM((tokens, model), BF16),
                pltpu.VMEM((fw, block), F32),
                pltpu.VMEM((T - 1, tokens - straight, model), BF16),
                dma((5,)), dma((4,)), dma((4 if block % 512 == 0 else 1,)),
                dma((1,)), dma((K,)), dma((1,)), dma((K,)),
                dma((T,)), dma((T,)),
                dma((T - 1, 2)), dma((T - 1, R)),
                dma((T - 1, K, 2)), dma((T - 1, K, R)),
                dma((T - 1, K, 2)), dma((T - 1, K, R)),
                dma((T,)), dma((T,)),
                dma((1,)), dma((1,)),
                dma((T,)), dma((T,)),
                dma((1,)), dma((K,)), dma((K, S - 1)), dma((K,)),
                dma((T,)), dma((T, K)),
                dma((T,)), dma((T, max(M - 1, 1))),
                dma((T - 1,)), dma((T - 1, turns)), dma((T - 1,)), dma((T - 1, turns)),
            ],
            compiler_params=pltpu.CompilerParams(
                collective_id=0, has_side_effects=True, vmem_limit_bytes=58 << 20
            ),
        )(
            in_flight[0, 0], segments, norm_gain, jnp.transpose(w_qkv[0], (1, 0, 2)), w_out[0],
            final_gain[None], student_rows[0], student_gain, w_head[0],
        )
        return adv[None, None], grad[None]

    in_specs = (
        P("section", "student", None, None),
        P(None, "student", None),
        P("section", None),
        P("section", None, None, "dp"),
        P("section", "dp", None),
        P(),
        P("student", None, None, "dp", None),
        P("student", None),
        P("student", None, "section"),
    )
    out_specs = (P("section", "student", "dp", None), P("student", "dp", "section"))
    return jax.shard_map(
        on_device, mesh=mesh, in_specs=in_specs, out_specs=out_specs, check_vma=False
    )
```

```python
import functools

import jax
import jax.numpy as jnp
from jax import lax
from jax.experimental import pallas as pl
from jax.experimental.pallas import tpu as pltpu
from jax.sharding import PartitionSpec as P

HEAD_SIZE = 128
LN_ROWS = 16
BF16 = jnp.bfloat16
F32 = jnp.float32
MESH = pl.DeviceIdType.MESH


def layer_norm(rows, gain):
    rows = rows.astype(F32)
    centred = rows - jnp.mean(rows, axis=-1, keepdims=True)
    spread = jnp.mean(centred * centred, axis=-1, keepdims=True)
    return centred * lax.rsqrt(spread + 1e-06) * gain


def attend(query, keys, values, same):
    scores = lax.dot_general(
        query, keys, (((1,), (1,)), ((), ())), preferred_element_type=F32
    ) * HEAD_SIZE ** (-0.5)
    scores = jnp.where(same, scores, -1e30)
    top = jnp.max(scores, axis=-1, keepdims=True)
    expo = jnp.exp(scores - top)
    probs = (expo / jnp.sum(expo, axis=-1, keepdims=True)).astype(BF16)
    return jnp.dot(probs, values, preferred_element_type=F32).astype(BF16)


def window_kernel(
    S, M, Z, T, pieces, turns,
    x_hbm, seg_ref, gain_ref, wqkv_ref, wout_ref, fgain_ref, srows_ref, sgain_ref, whead_ref,
    adv_ref, grad_ref,
    wqkv, wofull, whead, normed, xfull, mixfull, xs, xrows, fin, tg, tbuf, advbuf,
    sall, pred, fown, errs, x_ref, grad, det,
    local_sem, x_sem, out_sem, wo_s, wo_r, wf_s, wf_r, mx_s, mx_r, sh_s, sh_r, ar_s, ar_r, al_s, al_r,
    ro_s, ro_r, ad_s, ad_r, tg_s, tg_r, fe_s, fe_r, fp_s, fp_r,
    er_s, er_r, ml_s, ml_r, dz_s, dz_r, dx_s, dx_r,
):
    s = lax.axis_index("section")
    c = lax.axis_index("student")
    z = lax.axis_index("dp")
    root = S - 1
    tokens, model = x_ref.shape
    wid = wout_ref.shape[0]
    share = tokens // Z
    cw = model // Z
    block = whead_ref.shape[1]
    sw = whead_ref.shape[0]
    fw = sw // Z
    straight = tokens - det.shape[1]
    turn_rows = det.shape[1] // turns
    halves = 2 if M % 2 == 0 else 1
    part = c % halves
    hw = wid // halves
    sends = []
    owners = tuple(t if t < T - 1 and t < root else root for t in range(T))

    def remote(src, dst, send, recv, where):
        return pltpu.make_async_remote_copy(
            src_ref=src, dst_ref=dst, send_sem=send, recv_sem=recv,
            device_id=where, device_id_type=MESH,
        )

    def go(cond, build):
        if cond is True:
            build().start()
        else:
            pl.when(cond)(lambda: build().start())

    def owe(cond, ref, sem):
        sends.append((cond, lambda: remote(ref, ref, sem, sem, (s, c, zmod(z + 1)))))

    def landed(ref, sem):
        remote(ref, ref, sem, sem, (s, c, zmod(z + 1))).wait_recv()

    def post(cond, build):
        go(cond, build)
        sends.append((cond, build))

    def zmod(value):
        return lax.rem(value + Z, Z)

    def cols(index):
        return pl.ds(pl.multiple_of(index * cw, 128), cw)

    load_qkv = pltpu.make_async_copy(wqkv_ref, wqkv, local_sem.at[0])
    load_head = pltpu.make_async_copy(whead_ref, whead, local_sem.at[1])
    own_wo = pltpu.make_async_copy(
        wout_ref.at[:, cols(z)],
        wofull.at[pl.ds(pl.multiple_of(z * wid, wid), wid), :],
        local_sem.at[2],
    )
    xr = tokens // x_sem.shape[0]
    load_x = [
        pltpu.make_async_copy(
            x_hbm.at[pl.ds(i * xr, xr), :], x_ref.at[pl.ds(i * xr, xr), :], x_sem.at[i]
        )
        for i in range(x_sem.shape[0])
    ]
    load_rows = pltpu.make_async_copy(srows_ref, sall.at[0], local_sem.at[3])
    save_adv = pltpu.make_async_copy(advbuf, adv_ref, local_sem.at[4])

    barrier = pltpu.get_barrier_semaphore()

    def greet(where):
        pl.semaphore_signal(barrier, inc=1, device_id=where, device_id_type=MESH)

    for at in range(S):
        for k in range(Z):
            if k:
                greet((jnp.int32(at), c, zmod(z + k)))
            else:
                pl.when(s != at)(functools.partial(greet, (jnp.int32(at), c, z)))
        for dm in range(1, M):
            greet((jnp.int32(at), lax.rem(c + dm, M), z))
    for copy in load_x:
        copy.start()
    load_qkv.start()
    own_wo.start()
    load_rows.start()
    load_head.start()
    pl.semaphore_wait(barrier, S * Z - 1 + S * (M - 1))

    def wo_rows(source, which):
        return pl.ds(pl.multiple_of(source * wid + which * hw, hw), hw)

    for k in sorted(range(1, Z), reverse=True):
        def build(k=k):
            to = zmod(z + k)
            return remote(
                wout_ref.at[pl.ds(pl.multiple_of(part * hw, hw), hw), cols(to)],
                wofull.at[wo_rows(z, part), :],
                wo_s.at[0], wo_r.at[k - 1], (s, c, to),
            )
        go(True, build)
    owe(True, wofull.at[pl.ds(0, (Z - 1) * hw), :], wo_s.at[0])

    def pass_on(k):
        source = zmod(z - k)
        mine = wofull.at[wo_rows(source, part), :]
        mate = c + 1 - 2 * part
        return remote(mine, mine, wf_s.at[0], wf_r.at[k - 1], (s, mate, z))

    def gather_wo():
        for k in range(1, Z):
            source = zmod(z - k)
            mine = wofull.at[wo_rows(source, part), :]
            landed(mine, wo_r.at[k - 1])
            if halves == 2:
                go(True, functools.partial(pass_on, k))
        if halves == 2:
            owe(True, wofull.at[pl.ds(0, (Z - 1) * hw), :], wf_s.at[0])
            for k in range(1, Z):
                source = zmod(z - k)
                other = wofull.at[wo_rows(source, 1 - part), :]
                landed(other, wf_r.at[k - 1])
        own_wo.wait()

    handing = root > 1

    def slots(j):
        return (z >= j, j, z < Z - 1, z + 1), (z + j < Z, (Z - j) % Z, z > 0, z - 1)

    def send_rows(j):
        for way, (here, at, more, to) in enumerate(slots(j)):
            lands = (at + 1) % Z if way == 0 else (at + Z - 1) % Z

            def build(at=at, to=to, lands=lands, way=way):
                return remote(sall.at[at], sall.at[lands], fe_s.at[j, way], fe_r.at[lands - 1],
                              (s, c, to))
            post(jnp.logical_and(s == 0, jnp.logical_and(here, more)), build)

    def pass_rows():
        send_rows(0)
        for j in range(1, Z):
            for here, at, more, to in slots(j):
                mine = jnp.logical_and(s == 0, here)
                pl.when(mine)(functools.partial(landed, sall.at[at], fe_r.at[at - 1]))
            if j < Z - 1:
                send_rows(j)
            for here, at, more, to in slots(j):
                mine = jnp.logical_and(s == 0, here)
                for to in range(1, S):
                    def build(at=at, to=to):
                        there = sall.at[at]
                        return remote(there, there, fp_s.at[at - 1, to - 1], fp_r.at[at - 1],
                                      (jnp.int32(to), c, z))
                    if to != root or not handing:
                        post(mine, build)

    def hand_rows(j):
        for here, at, more, to in slots(j):
            there = sall.at[at]

            def build(at=at, there=there):
                return remote(there, there, fp_s.at[at - 1, root - 1], fp_r.at[at - 1],
                              (jnp.int32(root), c, z))
            if handing:
                mine = jnp.logical_and(s == 1, here)
                pl.when(mine)(functools.partial(landed, there, fp_r.at[at - 1]))
                post(mine, build)

    def student():
        for k in range(1, Z):
            pl.when(s > 1 if handing else s > 0)(
                functools.partial(landed, sall.at[k], fp_r.at[k - 1])
            )

        def one(k, carry):
            rows = layer_norm(sall[k].astype(F32).reshape(T * M * share, sw), sgain_ref[...])
            rows = rows.astype(BF16)
            for zz in range(Z):
                def own(zz=zz):
                    fown[k] = rows[:, zz * fw:(zz + 1) * fw].reshape(T, M * share, fw)
                pl.when(z == zz)(own)
            pred[k] = jnp.dot(rows, whead[...], preferred_element_type=F32).reshape(
                T, M, share, block
            )
            return carry

        lax.fori_loop(0, Z, one, 0)

    def spread(t, who):
        pl.when(jnp.logical_and(who, s != owners[t]))(
            functools.partial(landed, tbuf.at[t, c, 0], tg_r.at[t])
        )
        for k in range(1, Z):
            def build(k=k):
                return remote(tbuf.at[t, c, 0], tbuf.at[t, c, k], er_s.at[t],
                              er_r.at[t, k - 1], (s, c, zmod(z + k)))
            go(who, build)
        owe(who, tbuf.at[t, c, pl.ds(0, Z - 1)], er_s.at[t])

    def relay(t):
        for k in range(Z):
            there = tbuf.at[t, c, k]
            if k:
                landed(there, er_r.at[t, k - 1])
            for dm in range(1, M):
                def build(k=k, dm=dm):
                    there = tbuf.at[t, c, k]
                    return remote(there, there, ml_s.at[t], ml_r.at[t, dm - 1],
                                  (s, lax.rem(c + dm, M), z))
                go(True, build)
        if M > 1:
            owe(True, tbuf.at[t, pl.ds(0, M - 1)], ml_s.at[t])

    gw = block // out_sem.shape[0]

    def save_grad(j):
        at = pl.ds(j * gw, gw)
        return pltpu.make_async_copy(grad.at[:, at], grad_ref.at[:, at], out_sem.at[j])

    def gradient(t):
        for dm in range(1, M):
            landed(tbuf.at[t, lax.rem(c + M - dm, M)], ml_r.at[t, dm - 1])

        def one(k, carry):
            err = (pred[k, t] - tbuf[t, :, k].astype(F32)) * (2.0 / tokens)
            errs[k] = err.reshape(M * share, block).astype(BF16)
            return carry

        lax.fori_loop(0, Z, one, 0)
        feats = fown[:, t].reshape(Z * M * share, fw)
        for j in range(block // gw):
            at = slice(j * gw, (j + 1) * gw)
            term = lax.dot_general(
                feats, errs[:, :, at].reshape(Z * M * share, gw),
                (((0,), (0,)), ((), ())), preferred_element_type=F32,
            )
            if t == 0:
                grad[:, at] = term
            else:
                grad[:, at] += term
            if t == T - 1:
                save_grad(j).start()

    def turned(t):
        return root - (T - 1) + t

    def forward(t):
        cond = jnp.logical_and(s >= t, s + 1 <= turned(t + 1))
        for r in range(turns):
            at = pl.ds(r * turn_rows, turn_rows)

            def build(r=r, at=at):
                return remote(det.at[t, at, :],
                              xfull.at[t, pl.ds(straight + r * turn_rows, turn_rows), :],
                              dx_s.at[t], dx_r.at[t, r], (s + 1, c, z))
            whole = det.at[t, at, pl.ds(0, (Z - 1) * cw)]
            pl.when(cond)(functools.partial(landed, whole, dz_r.at[t, r]))
            go(cond, build)
        owe(cond, det.at[t], dx_s.at[t])

    def gather_state(t, active):
        all_straight = turned(t) < root

        def piece(r, origin):
            low, size = pieces[r]
            return xfull.at[t - 1, pl.ds(low, size), cols(origin)]

        def used(r):
            if pieces[r][0] < straight:
                return active
            return jnp.logical_and(active, s > turned(t))

        numbers = [r for r in range(len(pieces)) if pieces[r][0] < straight or all_straight]

        def to_right(r, k):
            there = piece(r, z - k)
            return remote(there, there, ar_s.at[t - 1, k, part_of(r)], ar_r.at[t - 1, k, r],
                          (s, c, z + 1))

        def to_left(r, k):
            there = piece(r, z + k)
            return remote(there, there, al_s.at[t - 1, k, part_of(r)], al_r.at[t - 1, k, r],
                          (s, c, z - 1))

        def part_of(r):
            return 0 if pieces[r][0] < straight else 1

        def send(cond, build, r, k, sem):
            go(jnp.logical_and(used(r), cond), functools.partial(build, r, k))
            size = straight if r == 0 else tokens - straight
            if r == 0 or part_of(r):
                owe(jnp.logical_and(used(r), cond),
                    xfull.at[t - 1, pl.ds(0, size), pl.ds(0, cw)], sem.at[t - 1, k, part_of(r)])

        for r in numbers:
            pl.when(used(r))(functools.partial(landed, piece(r, z), sh_r.at[t - 1, r]))
            send(z < Z - 1, to_right, r, 0, ar_s)
            send(z > 0, to_left, r, 0, al_s)
        if t == 1:
            forward(0)
        for k in range(1, Z):
            for r in numbers:
                pl.when(jnp.logical_and(used(r), z >= k))(
                    functools.partial(landed, piece(r, z - k), ar_r.at[t - 1, k - 1, r])
                )
                if k < Z - 1:
                    send(jnp.logical_and(z >= k, z < Z - 1), to_right, r, k, ar_s)
                pl.when(jnp.logical_and(used(r), z + k < Z))(
                    functools.partial(landed, piece(r, z + k), al_r.at[t - 1, k - 1, r])
                )
                if k < Z - 1:
                    send(jnp.logical_and(z + k < Z, z > 0), to_left, r, k, al_s)

        def turned_in():
            for r in range(turns):
                landed(xfull.at[t - 1, pl.ds(straight + r * turn_rows, turn_rows), :],
                       dx_r.at[t - 1, r])
        pl.when(jnp.logical_and(active, s <= turned(t)))(turned_in)

    def mix_cols(index):
        return pl.ds(pl.multiple_of(index * wid, 128), wid)

    def mixing(t):
        source = x_ref if t == 0 else xfull.at[t - 1]
        if t == 0:
            for copy in load_x:
                copy.wait()

        def norm_rows(i, carry):
            rows = pl.ds(pl.multiple_of(i * LN_ROWS, LN_ROWS), LN_ROWS)
            normed[rows, :] = layer_norm(source[rows, :], gain_ref[...]).astype(BF16)
            return carry

        lax.fori_loop(0, tokens // LN_ROWS, norm_rows, 0)
        if t == 0:
            load_qkv.wait()
        rows = normed[...]
        query, keys, values = [
            jnp.dot(rows, wqkv[j], preferred_element_type=F32).astype(BF16)
            for j in range(3)
        ]
        crops = jnp.broadcast_to(seg_ref[s - t].astype(F32), (tokens, tokens))
        same = crops == crops.T
        outs = []
        for h in range(wid // HEAD_SIZE):
            at = slice(h * HEAD_SIZE, (h + 1) * HEAD_SIZE)
            outs.append(attend(query[:, at], keys[:, at], values[:, at], same))
        mixfull[t, :, mix_cols(z)] = jnp.concatenate(outs, axis=1)

    def send_mixed(t, active):
        for k in range(1, Z):
            def build(k=k):
                own = mixfull.at[t, :, mix_cols(z)]
                return remote(own, own, mx_s.at[t], mx_r.at[t], (s, c, zmod(z + k)))
            go(active, build)
        owe(active, mixfull.at[t, :, pl.ds(0, (Z - 1) * wid)], mx_s.at[t])

    def project(t):
        landed(mixfull.at[t, :, pl.ds(0, (Z - 1) * wid)], mx_r.at[t])
        own = x_ref[:, cols(z)] if t == 0 else xfull[t - 1, :, cols(z)]
        summed = own.astype(F32) + jnp.dot(mixfull[t], wofull[...], preferred_element_type=F32)
        if t < T - 1:
            xs[t] = summed.astype(BF16)
            det[t, :, cols(z)] = summed[straight:].astype(BF16)
        xrows[t] = summed.reshape(Z, share, cw).astype(BF16)

    def send_state(t, active):
        if t < T - 1:
            go_on = jnp.logical_and(active, s < root)
            bend = jnp.logical_and(go_on, s + 1 <= turned(t + 1))
            for r in range(turns):
                for k in range(1, Z):
                    def build_turn(r=r, k=k):
                        there = det.at[t, pl.ds(r * turn_rows, turn_rows), cols(z)]
                        return remote(there, there, dz_s.at[t], dz_r.at[t, r],
                                      (s, c, zmod(z + k)))
                    go(bend, build_turn)
            owe(bend, det.at[t, :, pl.ds(0, (Z - 1) * cw)], dz_s.at[t])
            for r, (low, size) in enumerate(pieces):
                def build(r=r, low=low, size=size):
                    at = pl.ds(low, size)
                    return remote(xs.at[t, at, :], xfull.at[t, at, cols(z)],
                                  sh_s.at[t, 0 if low < straight else 1], sh_r.at[t, r],
                                  (s + 1, c, z))
                if low < straight:
                    go(go_on, build)
                elif turned(t + 1) < root:
                    post(jnp.logical_and(go_on, s + 1 > turned(t + 1)), build)
            owe(go_on, xs.at[t, pl.ds(0, straight), :], sh_s.at[t, 0])
        else:
            for k in range(Z):
                def build(k=k):
                    to = zmod(z + k)
                    return remote(xrows.at[t, to], advbuf.at[:, cols(z)],
                                  ad_s.at[0], ad_r.at[0], (s + 1, c, to))
                go(jnp.logical_and(active, s < root), build)
            owe(jnp.logical_and(active, s < root), advbuf, ad_s.at[0])
        low = 0 if owners[t] != root else 1
        for k in range(low, Z):
            def build_row(k=k):
                to = zmod(z + k)
                return remote(xrows.at[t, to], fin.at[t, :, cols(z)],
                              ro_s.at[t], ro_r.at[t], (jnp.int32(owners[t]), c, to))
            go(s == root, build_row)
        owe(s == root, fin.at[t, :, pl.ds(0, (Z - low) * cw)], ro_s.at[t])

    def finish(t):
        own = owners[t]

        def rows():
            if own == root:
                fin[t, :, cols(z)] = xrows[t, z]
            landed(fin.at[t, :, pl.ds(0, (Z - (own == root)) * cw)], ro_r.at[t])
            tg[t] = layer_norm(fin[t], fgain_ref[...]).astype(BF16)
            tbuf[t, c, 0] = tg[t, :, own * block:(own + 1) * block]

        pl.when(s == own)(rows)
        for to in range(S):
            if to != own:
                def build(to=to):
                    return remote(tg.at[t, :, to * block:(to + 1) * block], tbuf.at[t, c, 0],
                                  tg_s.at[t], tg_r.at[t], (jnp.int32(to), c, z))
                go(s == own, build)
        owe(s == own, tg.at[t, :, pl.ds(0, (S - 1) * block)], tg_s.at[t])

    def nothing():
        advbuf[...] = jnp.zeros_like(advbuf)
        save_adv.start()

    last, others = s == root, s != root
    for t in range(T):
        active = True if t == 0 else s >= t
        if t == 0:
            mixing(0)
        elif t == 1:
            finish(0)
            gather_state(1, active)
            pass_rows()
            spread(0, last)
            pl.when(active)(functools.partial(mixing, t))
        else:
            if t == T - 1:
                hand_rows(1)
            forward(t - 1)
            if t == T - 1:
                for j in range(2, Z - 1):
                    hand_rows(j)
            gather_state(t, jnp.logical_and(active, others))
            pl.when(active)(functools.partial(mixing, t))
        send_mixed(t, active)
        if t == 0:
            pl.when(s < T)(nothing)
            gather_wo()
            project(0)
        else:
            if t < T - 1:
                gather_state(t + 1, last)
            else:
                load_head.wait()
                for before in range(1, t):
                    finish(before)
                    spread(before, others)
                relay(0)
                if Z > 2:
                    hand_rows(Z - 1)
            pl.when(active)(functools.partial(project, t))
        send_state(t, active)
        if t == 0:
            load_rows.wait()
        elif t == 1:
            spread(0, others)

    finish(T - 1)
    spread(T - 1, last)
    for before in range(1, T - 1):
        spread(before, last)
    spread(T - 1, others)
    student()
    for before in range(1, T - 1):
        relay(before)
    for before in range(T - 1):
        gradient(before)
    relay(T - 1)
    gradient(T - 1)

    def arrived():
        landed(advbuf, ad_r.at[0])
        save_adv.start()

    pl.when(s >= T)(arrived)
    save_adv.wait()
    for j in range(block // gw):
        save_grad(j).wait()
    for cond, build in sends:
        if cond is True:
            build().wait_send()
        else:
            pl.when(cond)(lambda build=build: build().wait_send())


def solution(mesh):
    S, M, Z = mesh.shape["section"], mesh.shape["student"], mesh.shape["dp"]

    def on_device(
        in_flight, segments, norm_gain, w_qkv, w_out, final_gain, student_rows, student_gain, w_head
    ):
        tokens, model = in_flight.shape[2:]
        wid = w_out.shape[1]
        T, share = student_rows.shape[1], tokens // Z
        sw, block = w_head.shape[1:]
        cw, fw = model // Z, sw // Z
        grain = tokens // 8
        straight, turns = 5 * grain, 3
        pieces = ((0, 2 * grain), (2 * grain, 2 * grain), (4 * grain, grain), (straight, 3 * grain))
        R = len(pieces)
        vmem = pl.BlockSpec(memory_space=pltpu.VMEM)
        hbm = pl.BlockSpec(memory_space=pl.ANY)
        dma = pltpu.SemaphoreType.DMA
        K = max(Z - 1, 1)
        adv, grad = pl.pallas_call(
            functools.partial(window_kernel, S, M, Z, T, pieces, turns),
            out_shape=(
                jax.ShapeDtypeStruct((share, model), BF16),
                jax.ShapeDtypeStruct((fw, block), F32),
            ),
            in_specs=[hbm, vmem, vmem, hbm, hbm, vmem, hbm, vmem, hbm],
            out_specs=(hbm, hbm),
            scratch_shapes=[
                pltpu.VMEM((3, model, wid), BF16),
                pltpu.VMEM((Z * wid, cw), BF16),
                pltpu.VMEM((sw, block), BF16),
                pltpu.VMEM((tokens, model), BF16),
                pltpu.VMEM((T - 1, tokens, model), BF16),
                pltpu.VMEM((T, tokens, Z * wid), BF16),
                pltpu.VMEM((T - 1, tokens, cw), BF16),
                pltpu.VMEM((T, Z, share, cw), BF16),
                pltpu.VMEM((T, share, model), BF16),
                pltpu.VMEM((T, share, model), BF16),
                pltpu.VMEM((T, M, Z, share, block), BF16),
                pltpu.VMEM((share, model), BF16),
                pltpu.VMEM((Z, T, M, share, sw), BF16),
                pltpu.VMEM((Z, T, M, share, block), F32),
                pltpu.VMEM((Z, T, M * share, fw), BF16),
                pltpu.VMEM((Z, M * share, block), BF16),
                pltpu.VMEM((tokens, model), BF16),
                pltpu.VMEM((fw, block), F32),
                pltpu.VMEM((T - 1, tokens - straight, model), BF16),
                dma((5,)), dma((4,)), dma((4 if block % 512 == 0 else 1,)),
                dma((1,)), dma((K,)), dma((1,)), dma((K,)),
                dma((T,)), dma((T,)),
                dma((T - 1, 2)), dma((T - 1, R)),
                dma((T - 1, K, 2)), dma((T - 1, K, R)),
                dma((T - 1, K, 2)), dma((T - 1, K, R)),
                dma((T,)), dma((T,)),
                dma((1,)), dma((1,)),
                dma((T,)), dma((T,)),
                dma((K, 2)), dma((K,)), dma((K, S - 1)), dma((K,)),
                dma((T,)), dma((T, K)),
                dma((T,)), dma((T, max(M - 1, 1))),
                dma((T - 1,)), dma((T - 1, turns)), dma((T - 1,)), dma((T - 1, turns)),
            ],
            compiler_params=pltpu.CompilerParams(
                collective_id=0, has_side_effects=True, vmem_limit_bytes=58 << 20
            ),
        )(
            in_flight[0, 0], segments, norm_gain, jnp.transpose(w_qkv[0], (1, 0, 2)), w_out[0],
            final_gain[None], student_rows[0], student_gain, w_head[0],
        )
        return adv[None, None], grad[None]

    in_specs = (
        P("section", "student", None, None),
        P(None, "student", None),
        P("section", None),
        P("section", None, None, "dp"),
        P("section", "dp", None),
        P(),
        P("student", None, None, "dp", None),
        P("student", None),
        P("student", None, "section"),
    )
    out_specs = (P("section", "student", "dp", None), P("student", "dp", "section"))
    return jax.shard_map(
        on_device, mesh=mesh, in_specs=in_specs, out_specs=out_specs, check_vma=False
    )
```

```python
import functools

import jax
import jax.numpy as jnp
from jax import lax
from jax.experimental import pallas as pl
from jax.experimental.pallas import tpu as pltpu
from jax.sharding import PartitionSpec as P

HEAD_SIZE = 128
LN_ROWS = 16
BF16 = jnp.bfloat16
F32 = jnp.float32
MESH = pl.DeviceIdType.MESH


def layer_norm(rows, gain):
    rows = rows.astype(F32)
    centred = rows - jnp.mean(rows, axis=-1, keepdims=True)
    spread = jnp.mean(centred * centred, axis=-1, keepdims=True)
    return centred * lax.rsqrt(spread + 1e-06) * gain


def attend(query, keys, values, same):
    scores = lax.dot_general(
        query, keys, (((1,), (1,)), ((), ())), preferred_element_type=F32
    ) * HEAD_SIZE ** (-0.5)
    scores = jnp.where(same, scores, -1e30)
    top = jnp.max(scores, axis=-1, keepdims=True)
    expo = jnp.exp(scores - top)
    probs = (expo / jnp.sum(expo, axis=-1, keepdims=True)).astype(BF16)
    return jnp.dot(probs, values, preferred_element_type=F32).astype(BF16)


def window_kernel(
    S, M, Z, T, pieces, turns,
    x_hbm, seg_ref, gain_ref, wqkv_ref, wout_ref, fgain_ref, srows_ref, sgain_ref, whead_ref,
    adv_ref, grad_ref,
    wqkv, wofull, whead, normed, xfull, mixfull, xs, xrows, fin, tg, tbuf, advbuf,
    sall, pred, fown, errs, x_ref, grad, det, slim_grad,
    local_sem, x_sem, out_sem, wo_s, wo_r, wf_s, wf_r, mx_s, mx_r, sh_s, sh_r, ar_s, ar_r, al_s, al_r,
    ro_s, ro_r, ad_s, ad_r, tg_s, tg_r, fe_s, fe_r, fp_s, fp_r,
    er_s, er_r, ml_s, ml_r, dz_s, dz_r, dx_s, dx_r,
):
    s = lax.axis_index("section")
    c = lax.axis_index("student")
    z = lax.axis_index("dp")
    root = S - 1
    tokens, model = x_ref.shape
    wid = wout_ref.shape[0]
    share = tokens // Z
    cw = model // Z
    block = whead_ref.shape[1]
    sw = whead_ref.shape[0]
    fw = sw // Z
    cuts = tg_r.shape[1]
    slim = share // cuts
    straight = tokens - det.shape[1]
    turn_rows = det.shape[1] // turns
    halves = 2 if M % 2 == 0 else 1
    part = c % halves
    hw = wid // halves
    sends = []
    owners = tuple(t if t < T - 1 and t < root else root for t in range(T))

    def remote(src, dst, send, recv, where):
        return pltpu.make_async_remote_copy(
            src_ref=src, dst_ref=dst, send_sem=send, recv_sem=recv,
            device_id=where, device_id_type=MESH,
        )

    def go(cond, build):
        if cond is True:
            build().start()
        else:
            pl.when(cond)(lambda: build().start())

    def owe(cond, ref, sem):
        sends.append((cond, lambda: remote(ref, ref, sem, sem, (s, c, zmod(z + 1)))))

    def landed(ref, sem):
        remote(ref, ref, sem, sem, (s, c, zmod(z + 1))).wait_recv()

    def post(cond, build):
        go(cond, build)
        sends.append((cond, build))

    def zmod(value):
        return lax.rem(value + Z, Z)

    def cols(index):
        return pl.ds(pl.multiple_of(index * cw, 128), cw)

    load_qkv = pltpu.make_async_copy(wqkv_ref, wqkv, local_sem.at[0])
    load_head = pltpu.make_async_copy(whead_ref, whead, local_sem.at[1])
    own_wo = pltpu.make_async_copy(
        wout_ref.at[:, cols(z)],
        wofull.at[pl.ds(pl.multiple_of(z * wid, wid), wid), :],
        local_sem.at[2],
    )
    xr = tokens // x_sem.shape[0]
    load_x = [
        pltpu.make_async_copy(
            x_hbm.at[pl.ds(i * xr, xr), :], x_ref.at[pl.ds(i * xr, xr), :], x_sem.at[i]
        )
        for i in range(x_sem.shape[0])
    ]
    load_rows = pltpu.make_async_copy(srows_ref, sall.at[0], local_sem.at[3])
    save_adv = pltpu.make_async_copy(advbuf, adv_ref, local_sem.at[4])

    barrier = pltpu.get_barrier_semaphore()

    def greet(where):
        pl.semaphore_signal(barrier, inc=1, device_id=where, device_id_type=MESH)

    for at in range(S):
        for k in range(Z):
            if k:
                greet((jnp.int32(at), c, zmod(z + k)))
            else:
                pl.when(s != at)(functools.partial(greet, (jnp.int32(at), c, z)))
        for dm in range(1, M):
            greet((jnp.int32(at), lax.rem(c + dm, M), z))
    for copy in load_x:
        copy.start()
    load_qkv.start()
    own_wo.start()
    load_rows.start()
    load_head.start()
    pl.semaphore_wait(barrier, S * Z - 1 + S * (M - 1))

    def wo_rows(source, which):
        return pl.ds(pl.multiple_of(source * wid + which * hw, hw), hw)

    for k in sorted(range(1, Z), reverse=True):
        def build(k=k):
            to = zmod(z + k)
            return remote(
                wout_ref.at[pl.ds(pl.multiple_of(part * hw, hw), hw), cols(to)],
                wofull.at[wo_rows(z, part), :],
                wo_s.at[0], wo_r.at[k - 1], (s, c, to),
            )
        go(True, build)
    owe(True, wofull.at[pl.ds(0, (Z - 1) * hw), :], wo_s.at[0])

    def pass_on(k):
        source = zmod(z - k)
        mine = wofull.at[wo_rows(source, part), :]
        mate = c + 1 - 2 * part
        return remote(mine, mine, wf_s.at[0], wf_r.at[k - 1], (s, mate, z))

    def gather_wo():
        for k in range(1, Z):
            source = zmod(z - k)
            mine = wofull.at[wo_rows(source, part), :]
            landed(mine, wo_r.at[k - 1])
            if halves == 2:
                go(True, functools.partial(pass_on, k))
        if halves == 2:
            owe(True, wofull.at[pl.ds(0, (Z - 1) * hw), :], wf_s.at[0])
            for k in range(1, Z):
                source = zmod(z - k)
                other = wofull.at[wo_rows(source, 1 - part), :]
                landed(other, wf_r.at[k - 1])
        own_wo.wait()

    handing = root > 1

    def slots(j):
        return (z >= j, j, z < Z - 1, z + 1), (z + j < Z, (Z - j) % Z, z > 0, z - 1)

    def send_rows(j):
        for way, (here, at, more, to) in enumerate(slots(j)):
            lands = (at + 1) % Z if way == 0 else (at + Z - 1) % Z

            def build(at=at, to=to, lands=lands, way=way):
                return remote(sall.at[at], sall.at[lands], fe_s.at[j, way], fe_r.at[lands - 1],
                              (s, c, to))
            post(jnp.logical_and(s == 0, jnp.logical_and(here, more)), build)

    def pass_rows():
        send_rows(0)
        for j in range(1, Z):
            for here, at, more, to in slots(j):
                mine = jnp.logical_and(s == 0, here)
                pl.when(mine)(functools.partial(landed, sall.at[at], fe_r.at[at - 1]))
            if j < Z - 1:
                send_rows(j)
            for here, at, more, to in slots(j):
                mine = jnp.logical_and(s == 0, here)
                for to in range(1, S):
                    def build(at=at, to=to):
                        there = sall.at[at]
                        return remote(there, there, fp_s.at[at - 1, to - 1], fp_r.at[at - 1],
                                      (jnp.int32(to), c, z))
                    if to != root or not handing:
                        post(mine, build)

    def hand_rows(j):
        for here, at, more, to in slots(j):
            there = sall.at[at]

            def build(at=at, there=there):
                return remote(there, there, fp_s.at[at - 1, root - 1], fp_r.at[at - 1],
                              (jnp.int32(root), c, z))
            if handing:
                mine = jnp.logical_and(s == 1, here)
                pl.when(mine)(functools.partial(landed, there, fp_r.at[at - 1]))
                post(mine, build)

    def student():
        for k in range(1, Z):
            pl.when(s > 1 if handing else s > 0)(
                functools.partial(landed, sall.at[k], fp_r.at[k - 1])
            )

        def one(k, carry):
            rows = layer_norm(sall[k].astype(F32).reshape(T * M * share, sw), sgain_ref[...])
            rows = rows.astype(BF16)
            for zz in range(Z):
                def own(zz=zz):
                    fown[k] = rows[:, zz * fw:(zz + 1) * fw].reshape(T, M * share, fw)
                pl.when(z == zz)(own)
            pred[k] = jnp.dot(rows, whead[...], preferred_element_type=F32).reshape(
                T, M, share, block
            )
            return carry

        lax.fori_loop(0, Z, one, 0)

    def spread(t, who):
        for h in range(cuts):
            at = pl.ds(h * slim, slim)
            pl.when(jnp.logical_and(who, s != owners[t]))(
                functools.partial(landed, tbuf.at[t, c, 0, at], tg_r.at[t, h])
            )
            for k in range(1, Z):
                def build(k=k, at=at, h=h):
                    return remote(tbuf.at[t, c, 0, at], tbuf.at[t, c, k, at], er_s.at[t],
                                  er_r.at[t, k - 1, h], (s, c, zmod(z + k)))
                go(who, build)
        owe(who, tbuf.at[t, c, pl.ds(0, Z - 1)], er_s.at[t])

    def relay(t):
        for h in range(cuts):
            at = pl.ds(h * slim, slim)
            for k in range(Z):
                there = tbuf.at[t, c, k, at]
                if k:
                    landed(there, er_r.at[t, k - 1, h])
                for dm in range(1, M):
                    def build(there=there, dm=dm):
                        return remote(there, there, ml_s.at[t], ml_r.at[t, dm - 1],
                                      (s, lax.rem(c + dm, M), z))
                    go(True, build)
        if M > 1:
            owe(True, tbuf.at[t, pl.ds(0, M - 1)], ml_s.at[t])

    gw = block // out_sem.shape[0]

    def save_grad(j):
        at = pl.ds(j * gw, gw)
        return pltpu.make_async_copy(slim_grad.at[:, at], grad_ref.at[:, at], out_sem.at[j])

    def gradient(t):
        for dm in range(1, M):
            landed(tbuf.at[t, lax.rem(c + M - dm, M)], ml_r.at[t, dm - 1])

        def one(k, carry):
            err = (pred[k, t] - tbuf[t, :, k].astype(F32)) * (2.0 / tokens)
            errs[k] = err.reshape(M * share, block).astype(BF16)
            return carry

        lax.fori_loop(0, Z, one, 0)
        feats = fown[:, t].reshape(Z * M * share, fw)
        for j in range(block // gw):
            at = slice(j * gw, (j + 1) * gw)
            term = lax.dot_general(
                feats, errs[:, :, at].reshape(Z * M * share, gw),
                (((0,), (0,)), ((), ())), preferred_element_type=F32,
            )
            if t == 0:
                grad[:, at] = term
            elif t < T - 1:
                grad[:, at] += term
            else:
                slim_grad[:, at] = (grad[:, at] + term).astype(BF16)
                save_grad(j).start()

    def turned(t):
        return root - (T - 1) + t

    def forward(t):
        cond = jnp.logical_and(s >= t, s + 1 <= turned(t + 1))
        for r in range(turns):
            at = pl.ds(r * turn_rows, turn_rows)

            def build(r=r, at=at):
                return remote(det.at[t, at, :],
                              xfull.at[t, pl.ds(straight + r * turn_rows, turn_rows), :],
                              dx_s.at[t], dx_r.at[t, r], (s + 1, c, z))
            whole = det.at[t, at, pl.ds(0, (Z - 1) * cw)]
            pl.when(cond)(functools.partial(landed, whole, dz_r.at[t, r]))
            go(cond, build)
        owe(cond, det.at[t], dx_s.at[t])

    def norm(t, low, size):
        source = x_ref if t == 0 else xfull.at[t - 1]

        def norm_rows(i, carry):
            rows = pl.ds(pl.multiple_of(low + i * LN_ROWS, LN_ROWS), LN_ROWS)
            normed[rows, :] = layer_norm(source[rows, :], gain_ref[...]).astype(BF16)
            return carry

        lax.fori_loop(0, size // LN_ROWS, norm_rows, 0)

    def gather_state(t, active):
        all_straight = turned(t) < root

        def piece(r, origin):
            low, size = pieces[r]
            return xfull.at[t - 1, pl.ds(low, size), cols(origin)]

        def used(r):
            if pieces[r][0] < straight:
                return active
            return jnp.logical_and(active, s > turned(t))

        numbers = [r for r in range(len(pieces)) if pieces[r][0] < straight or all_straight]

        def to_right(r, k):
            there = piece(r, z - k)
            return remote(there, there, ar_s.at[t - 1, k, part_of(r)], ar_r.at[t - 1, k, r],
                          (s, c, z + 1))

        def to_left(r, k):
            there = piece(r, z + k)
            return remote(there, there, al_s.at[t - 1, k, part_of(r)], al_r.at[t - 1, k, r],
                          (s, c, z - 1))

        def part_of(r):
            return 0 if pieces[r][0] < straight else 1

        def send(cond, build, r, k, sem):
            go(jnp.logical_and(used(r), cond), functools.partial(build, r, k))
            size = straight if r == 0 else tokens - straight
            if r == 0 or part_of(r):
                owe(jnp.logical_and(used(r), cond),
                    xfull.at[t - 1, pl.ds(0, size), pl.ds(0, cw)], sem.at[t - 1, k, part_of(r)])

        for r in numbers:
            pl.when(used(r))(functools.partial(landed, piece(r, z), sh_r.at[t - 1, r]))
            send(z < Z - 1, to_right, r, 0, ar_s)
            send(z > 0, to_left, r, 0, al_s)
        if t == 1:
            forward(0)
        for k in range(1, Z):
            for r in numbers:
                pl.when(jnp.logical_and(used(r), z >= k))(
                    functools.partial(landed, piece(r, z - k), ar_r.at[t - 1, k - 1, r])
                )
                if k < Z - 1:
                    send(jnp.logical_and(z >= k, z < Z - 1), to_right, r, k, ar_s)
                pl.when(jnp.logical_and(used(r), z + k < Z))(
                    functools.partial(landed, piece(r, z + k), al_r.at[t - 1, k - 1, r])
                )
                if k < Z - 1:
                    send(jnp.logical_and(z + k < Z, z > 0), to_left, r, k, al_s)
                else:
                    pl.when(used(r))(functools.partial(norm, t, *pieces[r]))

        def turned_in():
            for r in range(turns):
                landed(xfull.at[t - 1, pl.ds(straight + r * turn_rows, turn_rows), :],
                       dx_r.at[t - 1, r])
                norm(t, straight + r * turn_rows, turn_rows)
        pl.when(jnp.logical_and(active, s <= turned(t)))(turned_in)

    def mix_cols(index):
        return pl.ds(pl.multiple_of(index * wid, 128), wid)

    def mixing(t):
        if t == 0:
            for copy in load_x:
                copy.wait()
            norm(0, 0, tokens)
        if t == 0:
            load_qkv.wait()
        rows = normed[...]
        query, keys, values = [
            jnp.dot(rows, wqkv[j], preferred_element_type=F32).astype(BF16)
            for j in range(3)
        ]
        crops = jnp.broadcast_to(seg_ref[s - t].astype(F32), (tokens, tokens))
        same = crops == crops.T
        outs = []
        for h in range(wid // HEAD_SIZE):
            at = slice(h * HEAD_SIZE, (h + 1) * HEAD_SIZE)
            outs.append(attend(query[:, at], keys[:, at], values[:, at], same))
        mixfull[t, :, mix_cols(z)] = jnp.concatenate(outs, axis=1)

    def send_mixed(t, active):
        for k in range(1, Z):
            def build(k=k):
                own = mixfull.at[t, :, mix_cols(z)]
                return remote(own, own, mx_s.at[t], mx_r.at[t], (s, c, zmod(z + k)))
            go(active, build)
        owe(active, mixfull.at[t, :, pl.ds(0, (Z - 1) * wid)], mx_s.at[t])

    def project(t):
        landed(mixfull.at[t, :, pl.ds(0, (Z - 1) * wid)], mx_r.at[t])
        own = x_ref[:, cols(z)] if t == 0 else xfull[t - 1, :, cols(z)]
        summed = own.astype(F32) + jnp.dot(mixfull[t], wofull[...], preferred_element_type=F32)
        if t < T - 1:
            xs[t] = summed.astype(BF16)
            det[t, :, cols(z)] = summed[straight:].astype(BF16)
        xrows[t] = summed.reshape(Z, share, cw).astype(BF16)

    def send_state(t, active):
        if t < T - 1:
            go_on = jnp.logical_and(active, s < root)
            bend = jnp.logical_and(go_on, s + 1 <= turned(t + 1))
            for r in range(turns):
                for k in range(1, Z):
                    def build_turn(r=r, k=k):
                        there = det.at[t, pl.ds(r * turn_rows, turn_rows), cols(z)]
                        return remote(there, there, dz_s.at[t], dz_r.at[t, r],
                                      (s, c, zmod(z + k)))
                    go(bend, build_turn)
            owe(bend, det.at[t, :, pl.ds(0, (Z - 1) * cw)], dz_s.at[t])
            for r, (low, size) in enumerate(pieces):
                def build(r=r, low=low, size=size):
                    at = pl.ds(low, size)
                    return remote(xs.at[t, at, :], xfull.at[t, at, cols(z)],
                                  sh_s.at[t, 0 if low < straight else 1], sh_r.at[t, r],
                                  (s + 1, c, z))
                if low < straight:
                    go(go_on, build)
                elif turned(t + 1) < root:
                    post(jnp.logical_and(go_on, s + 1 > turned(t + 1)), build)
            owe(go_on, xs.at[t, pl.ds(0, straight), :], sh_s.at[t, 0])
        else:
            for k in range(Z):
                def build(k=k):
                    to = zmod(z + k)
                    return remote(xrows.at[t, to], advbuf.at[:, cols(z)],
                                  ad_s.at[0], ad_r.at[0], (s + 1, c, to))
                go(jnp.logical_and(active, s < root), build)
            owe(jnp.logical_and(active, s < root), advbuf, ad_s.at[0])

    def retire(t):
        low = 0 if owners[t] != root else 1
        for h in range(cuts):
            at = pl.ds(h * slim, slim)
            for k in range(low, Z):
                def build(k=k, h=h, at=at):
                    to = zmod(z + k)
                    return remote(xrows.at[t, to, at], fin.at[t, at, cols(z)],
                                  ro_s.at[t], ro_r.at[t, h], (jnp.int32(owners[t]), c, to))
                go(s == root, build)
        owe(s == root, fin.at[t, :, pl.ds(0, (Z - low) * cw)], ro_s.at[t])

    def finish(t):
        own = owners[t]
        for h in range(cuts):
            at = pl.ds(h * slim, slim)

            def rows(at=at, h=h):
                if own == root:
                    fin[t, at, cols(z)] = xrows[t, z, at]
                landed(fin.at[t, at, pl.ds(0, (Z - (own == root)) * cw)], ro_r.at[t, h])
                tg[t, at] = layer_norm(fin[t, at], fgain_ref[...]).astype(BF16)
                tbuf[t, c, 0, at] = tg[t, at, own * block:(own + 1) * block]

            pl.when(s == own)(rows)
            for to in range(S):
                if to != own:
                    def build(to=to, at=at, h=h):
                        return remote(tg.at[t, at, to * block:(to + 1) * block],
                                      tbuf.at[t, c, 0, at], tg_s.at[t], tg_r.at[t, h],
                                      (jnp.int32(to), c, z))
                    go(s == own, build)
        owe(s == own, tg.at[t, :, pl.ds(0, (S - 1) * block)], tg_s.at[t])

    def nothing():
        advbuf[...] = jnp.zeros_like(advbuf)
        save_adv.start()

    last, others = s == root, s != root
    for t in range(T):
        active = True if t == 0 else s >= t
        if t == 0:
            mixing(0)
        elif t == 1:
            finish(0)
            gather_state(1, active)
            pass_rows()
            spread(0, last)
            pl.when(active)(functools.partial(mixing, t))
        else:
            if t == T - 1:
                hand_rows(1)
            forward(t - 1)
            if t == T - 1:
                for j in range(2, Z - 1):
                    hand_rows(j)
            gather_state(t, jnp.logical_and(active, others))
            pl.when(active)(functools.partial(mixing, t))
        send_mixed(t, active)
        if t == 0:
            pl.when(s < T)(nothing)
            gather_wo()
            project(0)
        else:
            if t < T - 1:
                gather_state(t + 1, last)
            else:
                load_head.wait()
                for before in range(1, t):
                    finish(before)
                    spread(before, others)
                relay(0)
                if Z > 2:
                    hand_rows(Z - 1)
                spread(t, others)
            pl.when(active)(functools.partial(project, t))
        send_state(t, active)
        retire(t)
        if t == 0:
            load_rows.wait()
        elif t == 1:
            spread(0, others)

    finish(T - 1)
    spread(T - 1, last)
    for before in range(1, T - 1):
        spread(before, last)
    student()
    for before in range(1, T - 1):
        relay(before)
    for before in range(T - 1):
        gradient(before)
    relay(T - 1)
    gradient(T - 1)

    def arrived():
        landed(advbuf, ad_r.at[0])
        save_adv.start()

    pl.when(s >= T)(arrived)
    save_adv.wait()
    for j in range(block // gw):
        save_grad(j).wait()
    for cond, build in sends:
        if cond is True:
            build().wait_send()
        else:
            pl.when(cond)(lambda build=build: build().wait_send())


def solution(mesh):
    S, M, Z = mesh.shape["section"], mesh.shape["student"], mesh.shape["dp"]

    def on_device(
        in_flight, segments, norm_gain, w_qkv, w_out, final_gain, student_rows, student_gain, w_head
    ):
        tokens, model = in_flight.shape[2:]
        wid = w_out.shape[1]
        T, share = student_rows.shape[1], tokens // Z
        sw, block = w_head.shape[1:]
        cw, fw = model // Z, sw // Z
        grain = tokens // 8
        straight, turns = 6 * grain, 2
        pieces = ((0, 2 * grain), (2 * grain, 2 * grain), (4 * grain, 2 * grain), (straight, 2 * grain))
        R = len(pieces)
        cuts = 2 if share % 32 == 0 else 1
        vmem = pl.BlockSpec(memory_space=pltpu.VMEM)
        hbm = pl.BlockSpec(memory_space=pl.ANY)
        dma = pltpu.SemaphoreType.DMA
        K = max(Z - 1, 1)
        adv, grad = pl.pallas_call(
            functools.partial(window_kernel, S, M, Z, T, pieces, turns),
            out_shape=(
                jax.ShapeDtypeStruct((share, model), BF16),
                jax.ShapeDtypeStruct((fw, block), BF16),
            ),
            in_specs=[hbm, vmem, vmem, hbm, hbm, vmem, hbm, vmem, hbm],
            out_specs=(hbm, hbm),
            scratch_shapes=[
                pltpu.VMEM((3, model, wid), BF16),
                pltpu.VMEM((Z * wid, cw), BF16),
                pltpu.VMEM((sw, block), BF16),
                pltpu.VMEM((tokens, model), BF16),
                pltpu.VMEM((T - 1, tokens, model), BF16),
                pltpu.VMEM((T, tokens, Z * wid), BF16),
                pltpu.VMEM((T - 1, tokens, cw), BF16),
                pltpu.VMEM((T, Z, share, cw), BF16),
                pltpu.VMEM((T, share, model), BF16),
                pltpu.VMEM((T, share, model), BF16),
                pltpu.VMEM((T, M, Z, share, block), BF16),
                pltpu.VMEM((share, model), BF16),
                pltpu.VMEM((Z, T, M, share, sw), BF16),
                pltpu.VMEM((Z, T, M, share, block), F32),
                pltpu.VMEM((Z, T, M * share, fw), BF16),
                pltpu.VMEM((Z, M * share, block), BF16),
                pltpu.VMEM((tokens, model), BF16),
                pltpu.VMEM((fw, block), F32),
                pltpu.VMEM((T - 1, tokens - straight, model), BF16),
                pltpu.VMEM((fw, block), BF16),
                dma((5,)), dma((4,)), dma((4 if block % 512 == 0 else 1,)),
                dma((1,)), dma((K,)), dma((1,)), dma((K,)),
                dma((T,)), dma((T,)),
                dma((T - 1, 2)), dma((T - 1, R)),
                dma((T - 1, K, 2)), dma((T - 1, K, R)),
                dma((T - 1, K, 2)), dma((T - 1, K, R)),
                dma((T,)), dma((T, cuts)),
                dma((1,)), dma((1,)),
                dma((T,)), dma((T, cuts)),
                dma((K, 2)), dma((K,)), dma((K, S - 1)), dma((K,)),
                dma((T,)), dma((T, K, cuts)),
                dma((T,)), dma((T, max(M - 1, 1))),
                dma((T - 1,)), dma((T - 1, turns)), dma((T - 1,)), dma((T - 1, turns)),
            ],
            compiler_params=pltpu.CompilerParams(
                collective_id=0, has_side_effects=True, vmem_limit_bytes=58 << 20
            ),
        )(
            in_flight[0, 0], segments, norm_gain, jnp.transpose(w_qkv[0], (1, 0, 2)), w_out[0],
            final_gain[None], student_rows[0], student_gain, w_head[0],
        )
        return adv[None, None], grad[None].astype(F32)

    in_specs = (
        P("section", "student", None, None),
        P(None, "student", None),
        P("section", None),
        P("section", None, None, "dp"),
        P("section", "dp", None),
        P(),
        P("student", None, None, "dp", None),
        P("student", None),
        P("student", None, "section"),
    )
    out_specs = (P("section", "student", "dp", None), P("student", "dp", "section"))
    return jax.shard_map(
        on_device, mesh=mesh, in_specs=in_specs, out_specs=out_specs, check_vma=False
    )
```
